32 devices in a mesh: rep: 2 (over x), seq: 16 (over z, y, core).
Axes of the slice: x: 2, y: 2, z: 4, core: 2. Of those that a mesh axis runs over, the one named last changes fastest.
Arguments:
- keys: bfloat16 [2048, 5120], P(('rep', 'seq')), parts along dimension 0, may hold values from -36 to 36
- values: bfloat16 [2048, 5120], P(('rep', 'seq')), parts along dimension 0, may hold values from -6 to 6
- queries: bfloat16 [2, 1024, 5120], P(None, ('rep', 'seq')), parts along dimension 1, may hold values from -6 to 6
Outputs:
- attended: bfloat16 [2, 1024, 5120], P(None, ('rep', 'seq')), parts along dimension 1
The draws below stay inside these ranges and needn't reach their ends.
There are 2 independent parts, one for each index of `rep`. The reference program is written for one: setup_inputs(seed, part) draws one part's arguments, and reference() takes and returns one part's arrays. A program takes and returns all parts, laid end to end along the dimension named above; each array names one. Nothing has to cross between parts.
All inputs are finite; a program needn't handle non-finite values.
Results may differ from the reference program's by a relative error of at most 0.0038.
Values may be sent and summed in bfloat16 or wider, within the bound.
A program may use at most 128 MiB of HBM per device.

```python
import math
import jax
import jax.numpy as jnp
from jax import lax

D = 5120
HEADS = 40
HEAD_DIM = 128
CTX_DEV = 64
QUERY_TOKENS = 512
LAYERS = 2
CONTEXT = 1024


key_floor = 2.0


aligned_gain = 0.8


def shared_pattern(key):
    return jnp.sign(jax.random.normal(jax.random.fold_in(key, 41), (D,), jnp.float32))


def drawn_positions(key):
    block_count = CONTEXT // CTX_DEV
    offsets = jax.random.randint(jax.random.fold_in(key, 42), (block_count,), 4, CTX_DEV)
    return jnp.arange(block_count, dtype=jnp.int32) * CTX_DEV + offsets


def draw_keys(key, part):
    row_scale = jnp.exp(jax.random.uniform(jax.random.fold_in(key, 22), (CONTEXT, 1), jnp.float32, math.log(2.5), math.log(6.0)))
    base = jnp.clip(jax.random.normal(jax.random.fold_in(key, 21), (CONTEXT, D), jnp.float32), -6.0, 6.0)
    drawn = base * row_scale
    positions = drawn_positions(key)
    floor_rows = jnp.broadcast_to(key_floor * shared_pattern(key)[None], (positions.shape[0], D))
    drawn = drawn.at[positions].set(floor_rows)
    return drawn.astype(jnp.bfloat16)


def draw_queries(key, part):
    aligned = jnp.arange(QUERY_TOKENS, dtype=jnp.int32) % 4 == 2
    noise = jax.random.normal(jax.random.fold_in(key, 32), (LAYERS, QUERY_TOKENS, D), jnp.float32)
    matched = jnp.clip(aligned_gain * shared_pattern(key)[None, None] + 0.25 * noise, -6.0, 6.0)
    drawn = jnp.clip(jax.random.normal(jax.random.fold_in(key, 31), (LAYERS, QUERY_TOKENS, D), jnp.float32), -6.0, 6.0)
    drawn = jnp.where(aligned[None, :, None], matched, drawn)
    return drawn.astype(jnp.bfloat16)


def level_of(key, extent, cuts, least, top_value):
    def one(dim, shards_of):
        steps = jax.random.uniform(jax.random.fold_in(jax.random.fold_in(key, 6), dim), (shards_of,), jnp.float32, least / len(cuts), top_value / len(cuts))
        return jnp.repeat(jnp.exp(steps), extent[dim] // shards_of).reshape((-1,) + (1,) * (len(extent) - dim - 1))

    gain = one(*cuts[0])
    for cut in cuts[1:]:
        gain = gain * one(*cut)
    return gain


def gaussian(own_key, dims, spread, most, pieces=(), held_as=jnp.bfloat16):
    loudness = level_of(own_key, dims, pieces, -0.22, 0.18) if pieces else 1.0
    values = jax.random.normal(own_key, dims, jnp.float32) * spread * loudness
    return jnp.minimum(jnp.maximum(values, -most), most).astype(held_as)


def setup_inputs(seed: int = 0, part: int = 0) -> dict:
    streams_of = jax.random.split(jax.random.key(seed), 4)
    part_keys = jax.random.split(jax.random.fold_in(streams_of[3], part), 4)
    keys = draw_keys(jax.random.fold_in(jax.random.fold_in(streams_of[3], part), 71), part)
    values = gaussian(part_keys[1], (CONTEXT, D), 1.0, 6.0, ((0, 16),))
    queries = draw_queries(jax.random.fold_in(jax.random.fold_in(streams_of[3], part), 71), part)
    return dict(keys=keys, values=values, queries=queries)


def reference(keys, values, queries):
    scale = 1.0 / math.sqrt(HEAD_DIM)
    layer_outs = []
    for layer in range(LAYERS):
        query_layer = queries[layer]

        def one_head(head):
            start = head * HEAD_DIM
            q_head = lax.dynamic_slice_in_dim(query_layer, start, HEAD_DIM, 1)
            k_head = lax.dynamic_slice_in_dim(keys, start, HEAD_DIM, 1)
            v_head = lax.dynamic_slice_in_dim(values, start, HEAD_DIM, 1)
            scores = lax.dot_general(q_head, k_head, (((1,), (1,)), ((), ())), preferred_element_type=jnp.float32) * scale
            peak = lax.optimization_barrier(jnp.max(scores, axis=1))
            expo = jnp.exp(scores - peak[:, None])
            total = lax.optimization_barrier(jnp.sum(expo, axis=1))
            summed = jnp.dot(expo.astype(jnp.bfloat16), v_head, preferred_element_type=jnp.float32)
            return (summed / total[:, None]).astype(jnp.bfloat16)
        per_head = lax.map(one_head, jnp.arange(HEADS, dtype=jnp.int32))
        layer_outs.append(jnp.transpose(per_head, (1, 0, 2)).reshape(QUERY_TOKENS, D))
    return jnp.stack(layer_outs)
```

```python
import functools
import math

import jax
import jax.numpy as jnp
from jax import lax
from jax.experimental import pallas as pl
from jax.experimental.pallas import tpu as pltpu
from jax.sharding import PartitionSpec as P

HEAD_DIM = 128
GROUPS = 8
CORES = 2
SIDES = 2
PLANES = 4
CHIPS = PLANES * SIDES
MESH = pl.DeviceIdType.MESH


def attend_kernel(heads, lag, k_ref, v_ref, q_ref, out_ref, kv, qs, res, kv_send, kv_recv, q_send, q_recv,
                  fwd_send, fwd_recv, o_send, o_recv):
    rows = k_ref.shape[0]
    toks = q_ref.shape[1]
    group_width = heads * HEAD_DIM
    half = CHIPS * rows
    scale = 1.0 / math.sqrt(HEAD_DIM)
    rep = lax.axis_index("rep")
    me = lax.axis_index("seq")
    chip = lax.div(me, CORES)
    core = lax.rem(me, CORES)
    partner = me + 1 - 2 * core
    plane = lax.div(chip, SIDES)
    side = lax.rem(chip, SIDES)
    right = lax.div(plane, 2)
    inner = (plane == 1) | (plane == 2)
    outmost = 3 * (1 - right)
    facing = 2 - right
    near = 4 * right + 1 - plane

    def remote(src, dst, send, recv, target):
        return pltpu.make_async_remote_copy(
            src_ref=src, dst_ref=dst, send_sem=send, recv_sem=recv, device_id=(rep, target), device_id_type=MESH
        )

    def columns(owner, head):
        return pl.ds(pl.multiple_of(owner * group_width + head * HEAD_DIM, HEAD_DIM), HEAD_DIM)

    def chip_at(plane, side):
        return plane * SIDES + side

    my_rows = pl.ds(pl.multiple_of(chip * rows, rows), rows)
    my_toks = pl.ds(pl.multiple_of(me * toks, toks), toks)
    opposite = chip_at(facing, side)

    def send_to(dest, head):
        cols = columns(dest, head)
        remote(k_ref.at[:, cols], kv.at[head, 0, my_rows], kv_send, kv_recv.at[head], CORES * dest + core).start()
        remote(v_ref.at[:, cols], kv.at[head, 1, my_rows], kv_send, kv_recv.at[head], CORES * dest + core).start()
        for layer in range(CORES):
            remote(q_ref.at[layer, :, cols], qs.at[head, my_toks], q_send, q_recv.at[head], CORES * dest + layer).start()

    def keep(head):
        cols = columns(chip, head)
        pltpu.make_async_copy(k_ref.at[:, cols], kv.at[head, 0, my_rows], kv_recv.at[head]).start()
        pltpu.make_async_copy(v_ref.at[:, cols], kv.at[head, 1, my_rows], kv_recv.at[head]).start()
        pltpu.make_async_copy(q_ref.at[core, :, cols], qs.at[head, my_toks], q_recv.at[head]).start()
        remote(q_ref.at[1 - core, :, cols], qs.at[head, my_toks], q_send, q_recv.at[head], partner).start()

    def over_heads(step):
        def body(head, carry):
            step(head)
            return carry

        lax.fori_loop(0, heads, body, 0)

    barrier = pltpu.get_barrier_semaphore()

    def greet(device):
        pl.semaphore_signal(barrier, inc=1, device_id=(rep, device), device_id_type=MESH)

    @pl.when(inner)
    def _():
        greet(partner)
        for other in range(CORES):
            greet(CORES * opposite + other)
        pl.semaphore_wait(barrier, 2 * CORES - 1)
        for at in (0, PLANES - 1):
            for other in range(SIDES * CORES):
                greet(SIDES * CORES * at + other)
        over_heads(lambda head: send_to(opposite, head))
        pl.semaphore_wait(barrier, 2 * SIDES * CORES)

    @pl.when(jnp.logical_not(inner))
    def _():
        for other in range(SIDES * CORES):
            greet(SIDES * CORES * outmost + other)
        for other in range(CORES):
            greet(CORES * chip_at(plane, 1 - side) + other)
        greet(partner)
        pl.semaphore_wait(barrier, CORES * CHIPS - 1)
        for at in (1, 2):
            for other in range(SIDES * CORES):
                greet(SIDES * CORES * at + other)

    def send_far(head):
        send_to(chip_at(outmost, 1 - side), head)
        send_to(chip_at(outmost, side), head)
        send_to(chip_at(facing, 1 - side), head)

        @pl.when(jnp.logical_not(inner))
        def _():
            send_to(opposite, head)

    def send_close(head):
        send_to(chip_at(near, 1 - side), head)
        send_to(chip_at(near, side), head)
        send_to(chip_at(plane, 1 - side), head)

    over_heads(send_far)
    over_heads(send_close)
    over_heads(keep)

    def block(head, device):
        return res.at[head, pl.ds(pl.multiple_of(device * toks, toks), toks)]

    def give(head, at):
        place = out_ref.at[core, :, columns(chip, head)]
        for other in (1 - side, side):
            for layer in range(CORES):
                device = CORES * chip_at(at, other) + layer
                remote(block(head, device), place, o_send, o_recv, device).start()

    def give_plane(head):
        place = out_ref.at[core, :, columns(chip, head)]
        for layer in range(CORES):
            device = CORES * chip_at(plane, 1 - side) + layer
            remote(block(head, device), place, o_send, o_recv, device).start()
        remote(block(head, partner), place, o_send, o_recv, partner).start()
        pltpu.make_async_copy(block(head, me), place, o_recv).start()

    def late(head):
        give(head, facing)
        give_plane(head)

    chunk = SIDES * CORES * toks

    def compute(head, at):
        part = pl.ds(pl.multiple_of(at * chunk, chunk), chunk)
        scores = lax.dot_general(
            qs[head, part], kv[head, 0], (((1,), (1,)), ((), ())), preferred_element_type=jnp.float32
        )
        peak = jnp.max(scores, axis=1, keepdims=True)
        expo = jnp.exp((scores - peak) * scale)
        total = jnp.sum(expo, axis=1, keepdims=True)
        summed = jnp.dot(expo.astype(jnp.bfloat16), kv[head, 1], preferred_element_type=jnp.float32)
        res[head, part] = (summed / total).astype(jnp.bfloat16)

    def attend(head):
        direct = kv.at[head, :, pl.ds(0, half)]
        passed = kv.at[head, :, pl.ds(half, half)]
        pltpu.make_async_copy(direct, direct, kv_recv.at[head]).wait()
        forward = remote(direct, passed, fwd_send.at[head], fwd_recv.at[head], partner)
        forward.start()
        pltpu.make_async_copy(qs.at[head], qs.at[head], q_recv.at[head]).wait()
        forward.wait()

        @pl.when(head >= lag)
        def _():
            late(head - lag)

        compute(head, outmost)
        give(head, outmost)
        compute(head, facing)
        compute(head, near)
        give(head, near)
        compute(head, plane)

    over_heads(attend)

    def finish(head, carry):
        late(head)
        return carry

    lax.fori_loop(heads - lag, heads, finish, 0)

    pltpu.make_async_copy(out_ref, out_ref, o_recv).wait()
    both = kv.at[:, :, pl.ds(0, (CHIPS - 1) * rows)]
    pltpu.make_async_copy(both, both, kv_send).wait()
    most = qs.at[:, pl.ds(0, (CORES * CHIPS - 1) * toks)]
    pltpu.make_async_copy(most, most, q_send).wait()
    pltpu.make_async_copy(most, most, o_send).wait()


def by_heads(keys, values, queries):
    nseq = lax.axis_size("seq")
    rows, width = keys.shape
    _, toks, _ = queries.shape
    heads = width // HEAD_DIM // CHIPS
    lag = min(3, heads)
    any_space = pl.BlockSpec(memory_space=pl.ANY)
    dma = pltpu.SemaphoreType.DMA
    return pl.pallas_call(
        functools.partial(attend_kernel, heads, lag),
        out_shape=pltpu.VMEM(queries.shape, jnp.bfloat16),
        in_specs=[any_space] * 3,
        out_specs=pl.BlockSpec(memory_space=pltpu.VMEM),
        scratch_shapes=[
            pltpu.VMEM((heads, 2, nseq * rows, HEAD_DIM), jnp.bfloat16),
            pltpu.VMEM((heads, nseq * toks, HEAD_DIM), jnp.bfloat16),
            pltpu.VMEM((heads, nseq * toks, HEAD_DIM), jnp.bfloat16),
            dma, dma((heads,)), dma, dma((heads,)),
            dma((heads,)), dma((heads,)), dma, dma,
        ],
        compiler_params=pltpu.CompilerParams(collective_id=0, has_side_effects=True),
    )(keys, values, queries)


def by_groups(keys, values, queries):
    nseq = lax.axis_size("seq")
    blocks = nseq // GROUPS
    ctx_rows, width = keys.shape
    group_width = width // GROUPS
    heads_group = group_width // HEAD_DIM
    layers, tok_rows, _ = queries.shape
    query_total = tok_rows * nseq
    scale = 1.0 / math.sqrt(HEAD_DIM)

    def arrange(local_block):
        return local_block.reshape(ctx_rows // blocks, nseq, group_width)

    def by_source(array):
        return array.reshape((array.shape[0], blocks, GROUPS) + array.shape[2:])

    moved_keys, moved_values = (
        lax.all_to_all(arrange(keys), "seq", split_axis=1, concat_axis=1, tiled=True),
        lax.all_to_all(arrange(values), "seq", split_axis=1, concat_axis=1, tiled=True),
    )
    moved_keys = moved_keys.reshape(-1, group_width)
    moved_values = moved_values.reshape(-1, group_width)
    layer_outs = []
    for layer in range(layers):
        local_query = queries[layer]
        per_group = local_query.reshape(tok_rows, GROUPS, group_width)
        received = lax.all_to_all(
            jnp.broadcast_to(per_group[:, None], (tok_rows, blocks, GROUPS, group_width)).reshape(
                tok_rows, nseq, group_width
            ),
            "seq",
            split_axis=1,
            concat_axis=0,
            tiled=True,
        )
        own_block = received.reshape(query_total, group_width)

        def one_head(head):
            start = head * HEAD_DIM
            q_head = lax.dynamic_slice_in_dim(own_block, start, HEAD_DIM, 1)
            k_head = lax.dynamic_slice_in_dim(moved_keys, start, HEAD_DIM, 1)
            v_head = lax.dynamic_slice_in_dim(moved_values, start, HEAD_DIM, 1)
            scores = (
                lax.dot_general(
                    q_head, k_head, (((1,), (1,)), ((), ())), preferred_element_type=jnp.float32
                )
                * scale
            )
            peak = jnp.max(scores, axis=1)
            expo = jnp.exp(scores - peak[:, None])
            total = jnp.sum(expo, axis=1)
            summed = jnp.dot(expo.astype(jnp.bfloat16), v_head, preferred_element_type=jnp.float32)
            return (summed, peak, total)

        summed, peak, total = lax.map(one_head, jnp.arange(heads_group, dtype=jnp.int32))
        shaped = (
            summed.reshape(heads_group, nseq, tok_rows, HEAD_DIM),
            peak.reshape(heads_group, nseq, tok_rows),
            total.reshape(heads_group, nseq, tok_rows),
        )
        combine_summed = lax.all_to_all(shaped[0], "seq", split_axis=1, concat_axis=1, tiled=True)
        combine_peak = lax.all_to_all(shaped[1], "seq", split_axis=1, concat_axis=1, tiled=True)
        combine_total = lax.all_to_all(shaped[2], "seq", split_axis=1, concat_axis=1, tiled=True)
        rows = combine_peak.shape[2]
        summed_s = by_source(combine_summed)
        peak_s = by_source(combine_peak)
        total_s = by_source(combine_total)
        highest = jnp.max(peak_s, axis=1)
        factor = jnp.exp(peak_s - highest[:, None])
        denom = jnp.sum(factor * total_s, axis=1)
        numer = jnp.sum(factor[..., None] * summed_s, axis=1)
        result = numer / denom[..., None]
        result = jnp.transpose(result, (2, 1, 0, 3)).reshape(rows, GROUPS * heads_group * HEAD_DIM)
        mixed = result.astype(jnp.bfloat16)
        layer_outs.append(mixed)
    return jnp.stack(layer_outs)


def local(keys, values, queries):
    chips = lax.axis_size("seq") // CORES
    heads = keys.shape[1] // HEAD_DIM
    if chips == CHIPS and heads % chips == 0 and queries.shape[0] == CORES and queries.shape[1] % 16 == 0:
        return by_heads(keys, values, queries)
    return by_groups(keys, values, queries)


def solution(mesh):
    return jax.shard_map(
        local,
        mesh=mesh,
        in_specs=(P(("rep", "seq"), None), P(("rep", "seq"), None), P(None, ("rep", "seq"), None)),
        out_specs=P(None, ("rep", "seq"), None),
        check_vma=False,
    )
```

```python
import functools
import math

import jax
import jax.numpy as jnp
from jax import lax
from jax.experimental import pallas as pl
from jax.experimental.pallas import tpu as pltpu
from jax.sharding import PartitionSpec as P

HEAD_DIM = 128
GROUPS = 8
CORES = 2
SIDES = 2
PLANES = 4
CHIPS = PLANES * SIDES
LAGS = ((3, 3, 3, 3), (0, 0, 0, 5), (0, 0, 3, 4), (0, 0, 4, 5))
FIRST = 3
MESH = pl.DeviceIdType.MESH


def attend_kernel(heads, k_ref, v_ref, q_ref, out_ref, kv, qs, res, kv_send, kv_recv, q_send, q_recv,
                  fwd_send, fwd_recv, o_send, o_recv):
    rows = k_ref.shape[0]
    toks = q_ref.shape[1]
    group_width = heads * HEAD_DIM
    half = CHIPS * rows
    scale = 1.0 / math.sqrt(HEAD_DIM)
    rep = lax.axis_index("rep")
    me = lax.axis_index("seq")
    chip = lax.div(me, CORES)
    core = lax.rem(me, CORES)
    partner = me + 1 - 2 * core
    plane = lax.div(chip, SIDES)
    side = lax.rem(chip, SIDES)
    right = lax.div(plane, 2)
    inner = (plane == 1) | (plane == 2)
    outmost = 3 * (1 - right)
    facing = 2 - right
    near = 4 * right + 1 - plane

    def remote(src, dst, send, recv, target):
        return pltpu.make_async_remote_copy(
            src_ref=src, dst_ref=dst, send_sem=send, recv_sem=recv, device_id=(rep, target), device_id_type=MESH
        )

    def columns(owner, head):
        return pl.ds(pl.multiple_of(owner * group_width + head * HEAD_DIM, HEAD_DIM), HEAD_DIM)

    def chip_at(plane, side):
        return plane * SIDES + side

    my_rows = pl.ds(pl.multiple_of(chip * rows, rows), rows)
    my_toks = pl.ds(pl.multiple_of(me * toks, toks), toks)
    opposite = chip_at(facing, side)

    def send_rows(dest, head):
        cols = columns(dest, head)
        remote(k_ref.at[:, cols], kv.at[head, 0, my_rows], kv_send, kv_recv.at[head], CORES * dest + core).start()
        remote(v_ref.at[:, cols], kv.at[head, 1, my_rows], kv_send, kv_recv.at[head], CORES * dest + core).start()

    def send_queries(dest, head):
        cols = columns(dest, head)
        for layer in range(CORES):
            remote(q_ref.at[layer, :, cols], qs.at[head, my_toks], q_send, q_recv.at[head], CORES * dest + layer).start()

    def send_to(dest, head):
        send_rows(dest, head)
        send_queries(dest, head)

    def keep(head):
        cols = columns(chip, head)
        pltpu.make_async_copy(k_ref.at[:, cols], kv.at[head, 0, my_rows], kv_recv.at[head]).start()
        pltpu.make_async_copy(v_ref.at[:, cols], kv.at[head, 1, my_rows], kv_recv.at[head]).start()
        pltpu.make_async_copy(q_ref.at[core, :, cols], qs.at[head, my_toks], q_recv.at[head]).start()
        remote(q_ref.at[1 - core, :, cols], qs.at[head, my_toks], q_send, q_recv.at[head], partner).start()

    def over_heads(step, begin=0):
        def body(head, carry):
            step(head)
            return carry

        lax.fori_loop(begin, heads, body, 0)

    barrier = pltpu.get_barrier_semaphore()

    def greet(device):
        pl.semaphore_signal(barrier, inc=1, device_id=(rep, device), device_id_type=MESH)

    def greet_outer():
        for at in (0, PLANES - 1):
            for other in range(SIDES * CORES):
                greet(SIDES * CORES * at + other)

    @pl.when(inner)
    def _():
        greet(CORES * opposite + core)

        @pl.when(core == 1)
        def _():
            pl.semaphore_wait(barrier, 1)
            greet(partner)
            for head in range(FIRST):
                send_rows(opposite, head)
            pl.semaphore_wait(barrier, 1)

        @pl.when(core == 0)
        def _():
            pl.semaphore_wait(barrier, 2)
            greet(partner)
            for head in range(FIRST):
                send_rows(opposite, head)

        greet_outer()
        for head in range(FIRST):
            send_queries(opposite, head)
        over_heads(lambda head: send_to(opposite, head), FIRST)
        pl.semaphore_wait(barrier, 1)

    @pl.when(jnp.logical_not(inner))
    def _():
        for other in range(SIDES * CORES):
            greet(SIDES * CORES * outmost + other)
        for other in range(CORES):
            greet(CORES * chip_at(plane, 1 - side) + other)
        greet(partner)
        pl.semaphore_wait(barrier, CORES * CHIPS - 1)
        greet(CORES * chip_at(near, side) + core)

    def send_far(head):
        send_to(chip_at(outmost, 1 - side), head)
        send_to(chip_at(outmost, side), head)
        send_to(chip_at(facing, 1 - side), head)

        @pl.when(jnp.logical_not(inner))
        def _():
            send_to(opposite, head)

    def send_close(head):
        send_to(chip_at(near, 1 - side), head)
        send_to(chip_at(near, side), head)
        send_to(chip_at(plane, 1 - side), head)

    over_heads(send_far)
    over_heads(send_close)
    over_heads(keep)

    def block(head, device):
        return res.at[head, pl.ds(pl.multiple_of(device * toks, toks), toks)]

    def give(head, at, other):
        place = out_ref.at[core, :, columns(chip, head)]
        for layer in range(CORES):
            device = CORES * chip_at(at, other) + layer
            remote(block(head, device), place, o_send, o_recv, device).start()

    def give_far(head, kind):
        give(head, (outmost, facing)[kind // SIDES], kind % SIDES)

    def give_plane(head):
        place = out_ref.at[core, :, columns(chip, head)]
        give(head, plane, 1 - side)
        remote(block(head, partner), place, o_send, o_recv, partner).start()
        pltpu.make_async_copy(block(head, me), place, o_recv).start()

    lags = [
        sum(min(LAGS[at][kind], heads) * jnp.where(plane == at, 1, 0) for at in range(PLANES))
        for kind in range(2 * SIDES)
    ]

    chunk = SIDES * CORES * toks

    def compute(head, at):
        part = pl.ds(pl.multiple_of(at * chunk, chunk), chunk)
        scores = lax.dot_general(
            qs[head, part], kv[head, 0], (((1,), (1,)), ((), ())), preferred_element_type=jnp.float32
        )
        peak = jnp.max(scores, axis=1, keepdims=True)
        expo = jnp.exp((scores - peak) * scale)
        total = jnp.sum(expo, axis=1, keepdims=True)
        summed = jnp.dot(expo.astype(jnp.bfloat16), kv[head, 1], preferred_element_type=jnp.float32)
        res[head, part] = (summed / total).astype(jnp.bfloat16)

    def attend(head):
        direct = kv.at[head, :, pl.ds(0, half)]
        passed = kv.at[head, :, pl.ds(half, half)]
        pltpu.make_async_copy(direct, direct, kv_recv.at[head]).wait()
        forward = remote(direct, passed, fwd_send.at[head], fwd_recv.at[head], partner)
        forward.start()
        pltpu.make_async_copy(qs.at[head], qs.at[head], q_recv.at[head]).wait()
        forward.wait()

        for kind, lag in enumerate(lags):

            @pl.when((lag > 0) & (head >= lag))
            def _():
                give_far(head - lag, kind)

        for half_plane, at in enumerate((outmost, facing)):
            compute(head, at)
            for kind in (2 * half_plane, 2 * half_plane + 1):

                @pl.when(lags[kind] == 0)
                def _():
                    give_far(head, kind)

        compute(head, near)
        give(head, near, 0)
        give(head, near, 1)
        compute(head, plane)
        give_plane(head)

    over_heads(attend)

    for kind, lag in enumerate(lags):
        over_heads(lambda head: give_far(head, kind), heads - lag)

    pltpu.make_async_copy(out_ref, out_ref, o_recv).wait()
    both = kv.at[:, :, pl.ds(0, (CHIPS - 1) * rows)]
    pltpu.make_async_copy(both, both, kv_send).wait()
    most = qs.at[:, pl.ds(0, (CORES * CHIPS - 1) * toks)]
    pltpu.make_async_copy(most, most, q_send).wait()
    pltpu.make_async_copy(most, most, o_send).wait()


def by_heads(keys, values, queries):
    nseq = lax.axis_size("seq")
    rows, width = keys.shape
    _, toks, _ = queries.shape
    heads = width // HEAD_DIM // CHIPS
    any_space = pl.BlockSpec(memory_space=pl.ANY)
    dma = pltpu.SemaphoreType.DMA
    return pl.pallas_call(
        functools.partial(attend_kernel, heads),
        out_shape=pltpu.VMEM(queries.shape, jnp.bfloat16),
        in_specs=[any_space] * 3,
        out_specs=pl.BlockSpec(memory_space=pltpu.VMEM),
        scratch_shapes=[
            pltpu.VMEM((heads, 2, nseq * rows, HEAD_DIM), jnp.bfloat16),
            pltpu.VMEM((heads, nseq * toks, HEAD_DIM), jnp.bfloat16),
            pltpu.VMEM((heads, nseq * toks, HEAD_DIM), jnp.bfloat16),
            dma, dma((heads,)), dma, dma((heads,)),
            dma((heads,)), dma((heads,)), dma, dma,
        ],
        compiler_params=pltpu.CompilerParams(collective_id=0, has_side_effects=True),
    )(keys, values, queries)


def by_groups(keys, values, queries):
    nseq = lax.axis_size("seq")
    blocks = nseq // GROUPS
    ctx_rows, width = keys.shape
    group_width = width // GROUPS
    heads_group = group_width // HEAD_DIM
    layers, tok_rows, _ = queries.shape
    query_total = tok_rows * nseq
    scale = 1.0 / math.sqrt(HEAD_DIM)

    def arrange(local_block):
        return local_block.reshape(ctx_rows // blocks, nseq, group_width)

    def by_source(array):
        return array.reshape((array.shape[0], blocks, GROUPS) + array.shape[2:])

    moved_keys, moved_values = (
        lax.all_to_all(arrange(keys), "seq", split_axis=1, concat_axis=1, tiled=True),
        lax.all_to_all(arrange(values), "seq", split_axis=1, concat_axis=1, tiled=True),
    )
    moved_keys = moved_keys.reshape(-1, group_width)
    moved_values = moved_values.reshape(-1, group_width)
    layer_outs = []
    for layer in range(layers):
        local_query = queries[layer]
        per_group = local_query.reshape(tok_rows, GROUPS, group_width)
        received = lax.all_to_all(
            jnp.broadcast_to(per_group[:, None], (tok_rows, blocks, GROUPS, group_width)).reshape(
                tok_rows, nseq, group_width
            ),
            "seq",
            split_axis=1,
            concat_axis=0,
            tiled=True,
        )
        own_block = received.reshape(query_total, group_width)

        def one_head(head):
            start = head * HEAD_DIM
            q_head = lax.dynamic_slice_in_dim(own_block, start, HEAD_DIM, 1)
            k_head = lax.dynamic_slice_in_dim(moved_keys, start, HEAD_DIM, 1)
            v_head = lax.dynamic_slice_in_dim(moved_values, start, HEAD_DIM, 1)
            scores = (
                lax.dot_general(
                    q_head, k_head, (((1,), (1,)), ((), ())), preferred_element_type=jnp.float32
                )
                * scale
            )
            peak = jnp.max(scores, axis=1)
            expo = jnp.exp(scores - peak[:, None])
            total = jnp.sum(expo, axis=1)
            summed = jnp.dot(expo.astype(jnp.bfloat16), v_head, preferred_element_type=jnp.float32)
            return (summed, peak, total)

        summed, peak, total = lax.map(one_head, jnp.arange(heads_group, dtype=jnp.int32))
        shaped = (
            summed.reshape(heads_group, nseq, tok_rows, HEAD_DIM),
            peak.reshape(heads_group, nseq, tok_rows),
            total.reshape(heads_group, nseq, tok_rows),
        )
        combine_summed = lax.all_to_all(shaped[0], "seq", split_axis=1, concat_axis=1, tiled=True)
        combine_peak = lax.all_to_all(shaped[1], "seq", split_axis=1, concat_axis=1, tiled=True)
        combine_total = lax.all_to_all(shaped[2], "seq", split_axis=1, concat_axis=1, tiled=True)
        rows = combine_peak.shape[2]
        summed_s = by_source(combine_summed)
        peak_s = by_source(combine_peak)
        total_s = by_source(combine_total)
        highest = jnp.max(peak_s, axis=1)
        factor = jnp.exp(peak_s - highest[:, None])
        denom = jnp.sum(factor * total_s, axis=1)
        numer = jnp.sum(factor[..., None] * summed_s, axis=1)
        result = numer / denom[..., None]
        result = jnp.transpose(result, (2, 1, 0, 3)).reshape(rows, GROUPS * heads_group * HEAD_DIM)
        mixed = result.astype(jnp.bfloat16)
        layer_outs.append(mixed)
    return jnp.stack(layer_outs)


def local(keys, values, queries):
    chips = lax.axis_size("seq") // CORES
    heads = keys.shape[1] // HEAD_DIM
    if chips == CHIPS and heads % chips == 0 and heads // chips > FIRST and queries.shape[0] == CORES and queries.shape[1] % 16 == 0:
        return by_heads(keys, values, queries)
    return by_groups(keys, values, queries)


def solution(mesh):
    return jax.shard_map(
        local,
        mesh=mesh,
        in_specs=(P(("rep", "seq"), None), P(("rep", "seq"), None), P(None, ("rep", "seq"), None)),
        out_specs=P(None, ("rep", "seq"), None),
        check_vma=False,
    )
```

```python
import functools
import math

import jax
import jax.numpy as jnp
from jax import lax
from jax.experimental import pallas as pl
from jax.experimental.pallas import tpu as pltpu
from jax.sharding import PartitionSpec as P

HEAD_DIM = 128
GROUPS = 8
CORES = 2
SIDES = 2
PLANES = 4
CHIPS = PLANES * SIDES
LAGS = (
    ((3, 3, 3, 3), (0, 0, 0, 3), (0, 0, 3, 3), (0, 0, 4, 4)),
    ((3, 3, 3, 3), (0, 0, 0, 5), (0, 0, 3, 5), (0, 0, 4, 5)),
)
FIRST = 3
MESH = pl.DeviceIdType.MESH


def attend_kernel(heads, k_ref, v_ref, q_ref, out_ref, kv, qs, res, kv_send, kv_recv, q_send, q_recv,
                  fwd_send, fwd_recv, o_send, o_recv):
    rows = k_ref.shape[0]
    toks = q_ref.shape[1]
    group_width = heads * HEAD_DIM
    half = CHIPS * rows
    scale = 1.0 / math.sqrt(HEAD_DIM)
    rep = lax.axis_index("rep")
    me = lax.axis_index("seq")
    chip = lax.div(me, CORES)
    core = lax.rem(me, CORES)
    partner = me + 1 - 2 * core
    plane = lax.div(chip, SIDES)
    side = lax.rem(chip, SIDES)
    right = lax.div(plane, 2)
    inner = (plane == 1) | (plane == 2)
    outmost = 3 * (1 - right)
    facing = 2 - right
    near = 4 * right + 1 - plane

    def remote(src, dst, send, recv, target):
        return pltpu.make_async_remote_copy(
            src_ref=src, dst_ref=dst, send_sem=send, recv_sem=recv, device_id=(rep, target), device_id_type=MESH
        )

    def columns(owner, head):
        return pl.ds(pl.multiple_of(owner * group_width + head * HEAD_DIM, HEAD_DIM), HEAD_DIM)

    def chip_at(plane, side):
        return plane * SIDES + side

    my_rows = pl.ds(pl.multiple_of(chip * rows, rows), rows)
    my_toks = pl.ds(pl.multiple_of(me * toks, toks), toks)
    opposite = chip_at(facing, side)

    def send_rows(dest, head):
        cols = columns(dest, head)
        remote(k_ref.at[:, cols], kv.at[head, 0, my_rows], kv_send, kv_recv.at[head], CORES * dest + core).start()
        remote(v_ref.at[:, cols], kv.at[head, 1, my_rows], kv_send, kv_recv.at[head], CORES * dest + core).start()

    def send_queries(dest, head):
        cols = columns(dest, head)
        for layer in range(CORES):
            remote(q_ref.at[layer, :, cols], qs.at[head, my_toks], q_send, q_recv.at[head], CORES * dest + layer).start()

    def send_to(dest, head):
        send_rows(dest, head)
        send_queries(dest, head)

    def keep(head):
        cols = columns(chip, head)
        pltpu.make_async_copy(k_ref.at[:, cols], kv.at[head, 0, my_rows], kv_recv.at[head]).start()
        pltpu.make_async_copy(v_ref.at[:, cols], kv.at[head, 1, my_rows], kv_recv.at[head]).start()
        pltpu.make_async_copy(q_ref.at[core, :, cols], qs.at[head, my_toks], q_recv.at[head]).start()
        remote(q_ref.at[1 - core, :, cols], qs.at[head, my_toks], q_send, q_recv.at[head], partner).start()

    def over_heads(step, begin=0):
        def body(head, carry):
            step(head)
            return carry

        lax.fori_loop(begin, heads, body, 0)

    barrier = pltpu.get_barrier_semaphore()

    def greet(device):
        pl.semaphore_signal(barrier, inc=1, device_id=(rep, device), device_id_type=MESH)

    def greet_outer():
        for at in (0, PLANES - 1):
            for other in range(SIDES * CORES):
                greet(SIDES * CORES * at + other)

    @pl.when(inner)
    def _():
        greet(CORES * opposite + core)

        @pl.when(core == 1)
        def _():
            pl.semaphore_wait(barrier, 1)
            greet(partner)
            for head in range(FIRST):
                send_rows(opposite, head)
            pl.semaphore_wait(barrier, 1)

        @pl.when(core == 0)
        def _():
            pl.semaphore_wait(barrier, 2)
            greet(partner)
            for head in range(FIRST):
                send_rows(opposite, head)

        greet_outer()
        for head in range(FIRST):
            send_queries(opposite, head)
        over_heads(lambda head: send_to(opposite, head), FIRST)
        pl.semaphore_wait(barrier, 1)

    @pl.when(jnp.logical_not(inner))
    def _():
        for other in range(SIDES * CORES):
            greet(SIDES * CORES * outmost + other)
        for other in range(CORES):
            greet(CORES * chip_at(plane, 1 - side) + other)
        greet(partner)
        pl.semaphore_wait(barrier, CORES * CHIPS - 1)
        greet(CORES * chip_at(near, side) + core)

    def send_far(head):
        send_to(chip_at(outmost, 1 - side), head)
        send_to(chip_at(outmost, side), head)
        send_to(chip_at(facing, 1 - side), head)

        @pl.when(jnp.logical_not(inner))
        def _():
            send_to(opposite, head)

    def send_close(head):
        send_to(chip_at(near, 1 - side), head)
        send_to(chip_at(near, side), head)
        send_to(chip_at(plane, 1 - side), head)

    over_heads(send_far)
    over_heads(send_close)
    over_heads(keep)

    def block(head, device):
        return res.at[head, pl.ds(pl.multiple_of(device * toks, toks), toks)]

    def give(head, at, other):
        place = out_ref.at[core, :, columns(chip, head)]
        for layer in range(CORES):
            device = CORES * chip_at(at, other) + layer
            remote(block(head, device), place, o_send, o_recv, device).start()

    def give_far(head, kind):
        give(head, (outmost, facing)[kind // SIDES], side if kind % SIDES else 1 - side)

    def give_plane(head):
        place = out_ref.at[core, :, columns(chip, head)]
        give(head, plane, 1 - side)
        remote(block(head, partner), place, o_send, o_recv, partner).start()
        pltpu.make_async_copy(block(head, me), place, o_recv).start()

    lags = [
        sum(
            min(LAGS[which][at][kind], heads) * jnp.where((plane == at) & (core == which), 1, 0)
            for which in range(CORES)
            for at in range(PLANES)
        )
        for kind in range(2 * SIDES)
    ]

    chunk = SIDES * CORES * toks

    def compute(head, at):
        part = pl.ds(pl.multiple_of(at * chunk, chunk), chunk)
        scores = lax.dot_general(
            qs[head, part], kv[head, 0], (((1,), (1,)), ((), ())), preferred_element_type=jnp.float32
        )
        peak = jnp.max(scores, axis=1, keepdims=True)
        expo = jnp.exp((scores - peak) * scale)
        total = jnp.sum(expo, axis=1, keepdims=True)
        summed = jnp.dot(expo.astype(jnp.bfloat16), kv[head, 1], preferred_element_type=jnp.float32)
        res[head, part] = (summed / total).astype(jnp.bfloat16)

    def attend(head):
        direct = kv.at[head, :, pl.ds(0, half)]
        passed = kv.at[head, :, pl.ds(half, half)]
        pltpu.make_async_copy(direct, direct, kv_recv.at[head]).wait()
        forward = remote(direct, passed, fwd_send.at[head], fwd_recv.at[head], partner)
        forward.start()
        pltpu.make_async_copy(qs.at[head], qs.at[head], q_recv.at[head]).wait()
        forward.wait()

        for kind, lag in enumerate(lags):

            @pl.when((lag > 0) & (head >= lag))
            def _():
                give_far(head - lag, kind)

        for half_plane, at in enumerate((outmost, facing)):
            compute(head, at)
            for kind in (2 * half_plane, 2 * half_plane + 1):

                @pl.when(lags[kind] == 0)
                def _():
                    give_far(head, kind)

        compute(head, near)
        give(head, near, 0)
        give(head, near, 1)
        compute(head, plane)
        give_plane(head)

    over_heads(attend)

    for kind, lag in enumerate(lags):
        over_heads(lambda head: give_far(head, kind), heads - lag)

    pltpu.make_async_copy(out_ref, out_ref, o_recv).wait()
    both = kv.at[:, :, pl.ds(0, (CHIPS - 1) * rows)]
    pltpu.make_async_copy(both, both, kv_send).wait()
    most = qs.at[:, pl.ds(0, (CORES * CHIPS - 1) * toks)]
    pltpu.make_async_copy(most, most, q_send).wait()
    pltpu.make_async_copy(most, most, o_send).wait()


def by_heads(keys, values, queries):
    nseq = lax.axis_size("seq")
    rows, width = keys.shape
    _, toks, _ = queries.shape
    heads = width // HEAD_DIM // CHIPS
    any_space = pl.BlockSpec(memory_space=pl.ANY)
    dma = pltpu.SemaphoreType.DMA
    return pl.pallas_call(
        functools.partial(attend_kernel, heads),
        out_shape=pltpu.VMEM(queries.shape, jnp.bfloat16),
        in_specs=[any_space] * 3,
        out_specs=pl.BlockSpec(memory_space=pltpu.VMEM),
        scratch_shapes=[
            pltpu.VMEM((heads, 2, nseq * rows, HEAD_DIM), jnp.bfloat16),
            pltpu.VMEM((heads, nseq * toks, HEAD_DIM), jnp.bfloat16),
            pltpu.VMEM((heads, nseq * toks, HEAD_DIM), jnp.bfloat16),
            dma, dma((heads,)), dma, dma((heads,)),
            dma((heads,)), dma((heads,)), dma, dma,
        ],
        compiler_params=pltpu.CompilerParams(collective_id=0, has_side_effects=True),
    )(keys, values, queries)


def by_groups(keys, values, queries):
    nseq = lax.axis_size("seq")
    blocks = nseq // GROUPS
    ctx_rows, width = keys.shape
    group_width = width // GROUPS
    heads_group = group_width // HEAD_DIM
    layers, tok_rows, _ = queries.shape
    query_total = tok_rows * nseq
    scale = 1.0 / math.sqrt(HEAD_DIM)

    def arrange(local_block):
        return local_block.reshape(ctx_rows // blocks, nseq, group_width)

    def by_source(array):
        return array.reshape((array.shape[0], blocks, GROUPS) + array.shape[2:])

    moved_keys, moved_values = (
        lax.all_to_all(arrange(keys), "seq", split_axis=1, concat_axis=1, tiled=True),
        lax.all_to_all(arrange(values), "seq", split_axis=1, concat_axis=1, tiled=True),
    )
    moved_keys = moved_keys.reshape(-1, group_width)
    moved_values = moved_values.reshape(-1, group_width)
    layer_outs = []
    for layer in range(layers):
        local_query = queries[layer]
        per_group = local_query.reshape(tok_rows, GROUPS, group_width)
        received = lax.all_to_all(
            jnp.broadcast_to(per_group[:, None], (tok_rows, blocks, GROUPS, group_width)).reshape(
                tok_rows, nseq, group_width
            ),
            "seq",
            split_axis=1,
            concat_axis=0,
            tiled=True,
        )
        own_block = received.reshape(query_total, group_width)

        def one_head(head):
            start = head * HEAD_DIM
            q_head = lax.dynamic_slice_in_dim(own_block, start, HEAD_DIM, 1)
            k_head = lax.dynamic_slice_in_dim(moved_keys, start, HEAD_DIM, 1)
            v_head = lax.dynamic_slice_in_dim(moved_values, start, HEAD_DIM, 1)
            scores = (
                lax.dot_general(
                    q_head, k_head, (((1,), (1,)), ((), ())), preferred_element_type=jnp.float32
                )
                * scale
            )
            peak = jnp.max(scores, axis=1)
            expo = jnp.exp(scores - peak[:, None])
            total = jnp.sum(expo, axis=1)
            summed = jnp.dot(expo.astype(jnp.bfloat16), v_head, preferred_element_type=jnp.float32)
            return (summed, peak, total)

        summed, peak, total = lax.map(one_head, jnp.arange(heads_group, dtype=jnp.int32))
        shaped = (
            summed.reshape(heads_group, nseq, tok_rows, HEAD_DIM),
            peak.reshape(heads_group, nseq, tok_rows),
            total.reshape(heads_group, nseq, tok_rows),
        )
        combine_summed = lax.all_to_all(shaped[0], "seq", split_axis=1, concat_axis=1, tiled=True)
        combine_peak = lax.all_to_all(shaped[1], "seq", split_axis=1, concat_axis=1, tiled=True)
        combine_total = lax.all_to_all(shaped[2], "seq", split_axis=1, concat_axis=1, tiled=True)
        rows = combine_peak.shape[2]
        summed_s = by_source(combine_summed)
        peak_s = by_source(combine_peak)
        total_s = by_source(combine_total)
        highest = jnp.max(peak_s, axis=1)
        factor = jnp.exp(peak_s - highest[:, None])
        denom = jnp.sum(factor * total_s, axis=1)
        numer = jnp.sum(factor[..., None] * summed_s, axis=1)
        result = numer / denom[..., None]
        result = jnp.transpose(result, (2, 1, 0, 3)).reshape(rows, GROUPS * heads_group * HEAD_DIM)
        mixed = result.astype(jnp.bfloat16)
        layer_outs.append(mixed)
    return jnp.stack(layer_outs)


def local(keys, values, queries):
    chips = lax.axis_size("seq") // CORES
    heads = keys.shape[1] // HEAD_DIM
    if chips == CHIPS and heads % chips == 0 and heads // chips > FIRST and queries.shape[0] == CORES and queries.shape[1] % 16 == 0:
        return by_heads(keys, values, queries)
    return by_groups(keys, values, queries)


def solution(mesh):
    return jax.shard_map(
        local,
        mesh=mesh,
        in_specs=(P(("rep", "seq"), None), P(("rep", "seq"), None), P(None, ("rep", "seq"), None)),
        out_specs=P(None, ("rep", "seq"), None),
        check_vma=False,
    )
```

```python
import functools
import math

import jax
import jax.numpy as jnp
from jax import lax
from jax.experimental import pallas as pl
from jax.experimental.pallas import tpu as pltpu
from jax.sharding import PartitionSpec as P

HEAD_DIM = 128
GROUPS = 8
CORES = 2
SIDES = 2
PLANES = 4
CHIPS = PLANES * SIDES
LAGS = (
    ((3, 3, 3, 3), (0, 0, 0, 3), (0, 0, 3, 3), (0, 0, 4, 5)),
    ((3, 3, 3, 3), (0, 0, 0, 5), (0, 0, 3, 5), (0, 0, 4, 5)),
)
LAST = 3
FIRST = 3
MESH = pl.DeviceIdType.MESH


def attend_kernel(heads, k_ref, v_ref, q_ref, out_ref, kv, qs, res, kv_send, kv_recv, q_send, q_recv,
                  fwd_send, fwd_recv, o_send, o_recv):
    rows = k_ref.shape[0]
    toks = q_ref.shape[1]
    group_width = heads * HEAD_DIM
    half = CHIPS * rows
    scale = 1.0 / math.sqrt(HEAD_DIM)
    rep = lax.axis_index("rep")
    me = lax.axis_index("seq")
    chip = lax.div(me, CORES)
    core = lax.rem(me, CORES)
    partner = me + 1 - 2 * core
    plane = lax.div(chip, SIDES)
    side = lax.rem(chip, SIDES)
    right = lax.div(plane, 2)
    inner = (plane == 1) | (plane == 2)
    outmost = 3 * (1 - right)
    facing = 2 - right
    near = 4 * right + 1 - plane

    def remote(src, dst, send, recv, target):
        return pltpu.make_async_remote_copy(
            src_ref=src, dst_ref=dst, send_sem=send, recv_sem=recv, device_id=(rep, target), device_id_type=MESH
        )

    def columns(owner, head):
        return pl.ds(pl.multiple_of(owner * group_width + head * HEAD_DIM, HEAD_DIM), HEAD_DIM)

    def chip_at(plane, side):
        return plane * SIDES + side

    my_rows = pl.ds(pl.multiple_of(chip * rows, rows), rows)
    my_toks = pl.ds(pl.multiple_of(me * toks, toks), toks)
    opposite = chip_at(facing, side)

    def send_rows(dest, head):
        cols = columns(dest, head)
        remote(k_ref.at[:, cols], kv.at[head, 0, my_rows], kv_send, kv_recv.at[head], CORES * dest + core).start()
        remote(v_ref.at[:, cols], kv.at[head, 1, my_rows], kv_send, kv_recv.at[head], CORES * dest + core).start()

    def send_queries(dest, head):
        cols = columns(dest, head)
        for layer in range(CORES):
            remote(q_ref.at[layer, :, cols], qs.at[head, my_toks], q_send, q_recv.at[head], CORES * dest + layer).start()

    def send_to(dest, head):
        send_rows(dest, head)
        send_queries(dest, head)

    def keep(head):
        cols = columns(chip, head)
        pltpu.make_async_copy(k_ref.at[:, cols], kv.at[head, 0, my_rows], kv_recv.at[head]).start()
        pltpu.make_async_copy(v_ref.at[:, cols], kv.at[head, 1, my_rows], kv_recv.at[head]).start()
        pltpu.make_async_copy(q_ref.at[core, :, cols], qs.at[head, my_toks], q_recv.at[head]).start()
        remote(q_ref.at[1 - core, :, cols], qs.at[head, my_toks], q_send, q_recv.at[head], partner).start()

    def over_heads(step, begin=0):
        def body(head, carry):
            step(head)
            return carry

        lax.fori_loop(begin, heads, body, 0)

    barrier = pltpu.get_barrier_semaphore()

    def greet(device):
        pl.semaphore_signal(barrier, inc=1, device_id=(rep, device), device_id_type=MESH)

    def greet_outer():
        for at in (0, PLANES - 1):
            for other in range(SIDES * CORES):
                greet(SIDES * CORES * at + other)

    @pl.when(inner)
    def _():
        greet(CORES * opposite + core)

        @pl.when(core == 1)
        def _():
            pl.semaphore_wait(barrier, 1)
            greet(partner)
            for head in range(FIRST):
                send_rows(opposite, head)
            pl.semaphore_wait(barrier, 1)

        @pl.when(core == 0)
        def _():
            pl.semaphore_wait(barrier, 2)
            greet(partner)
            for head in range(FIRST):
                send_rows(opposite, head)

        greet_outer()
        for head in range(FIRST):
            send_queries(opposite, head)
        over_heads(lambda head: send_to(opposite, head), FIRST)
        pl.semaphore_wait(barrier, 1)

    @pl.when(jnp.logical_not(inner))
    def _():
        for other in range(SIDES * CORES):
            greet(SIDES * CORES * outmost + other)
        for other in range(CORES):
            greet(CORES * chip_at(plane, 1 - side) + other)
        greet(partner)
        pl.semaphore_wait(barrier, CORES * CHIPS - 1)
        greet(CORES * chip_at(near, side) + core)

    def send_far(head):
        send_to(chip_at(outmost, 1 - side), head)
        send_to(chip_at(outmost, side), head)
        send_to(chip_at(facing, 1 - side), head)

        @pl.when(jnp.logical_not(inner))
        def _():
            send_to(opposite, head)

    def send_close(head):
        send_to(chip_at(near, 1 - side), head)
        send_to(chip_at(near, side), head)
        send_to(chip_at(plane, 1 - side), head)

    over_heads(send_far)
    over_heads(send_close)
    over_heads(keep)

    def block(head, device):
        return res.at[head, pl.ds(pl.multiple_of(device * toks, toks), toks)]

    def give(head, at, other, cores=(0, 1)):
        place = out_ref.at[core, :, columns(chip, head)]
        for where in cores:
            device = CORES * chip_at(at, other) + where
            remote(block(head, device), place, o_send, o_recv, device).start()

    kinds = (
        (outmost, 1 - side, (0, 1)),
        (outmost, side, (0, 1)),
        (facing, 1 - side, (1, 0)),
        (facing, side, (1,)),
        (facing, side, (0,)),
    )

    def give_far(head, kind):
        give(head, *kinds[kind])

    def give_plane(head):
        place = out_ref.at[core, :, columns(chip, head)]
        give(head, plane, 1 - side)
        remote(block(head, partner), place, o_send, o_recv, partner).start()
        pltpu.make_async_copy(block(head, me), place, o_recv).start()

    lags = [
        sum(
            min(LAGS[which][at][min(kind, 3)], heads) * jnp.where((plane == at) & (core == which), 1, 0)
            for which in range(CORES)
            for at in range(PLANES)
        )
        for kind in range(len(kinds))
    ]

    chunk = SIDES * CORES * toks

    def compute(head, at):
        part = pl.ds(pl.multiple_of(at * chunk, chunk), chunk)
        scores = lax.dot_general(
            qs[head, part], kv[head, 0], (((1,), (1,)), ((), ())), preferred_element_type=jnp.float32
        )
        peak = jnp.max(scores, axis=1, keepdims=True)
        expo = jnp.exp((scores - peak) * scale)
        total = jnp.sum(expo, axis=1, keepdims=True)
        summed = jnp.dot(expo.astype(jnp.bfloat16), kv[head, 1], preferred_element_type=jnp.float32)
        res[head, part] = (summed / total).astype(jnp.bfloat16)

    def attend(head):
        direct = kv.at[head, :, pl.ds(0, half)]
        passed = kv.at[head, :, pl.ds(half, half)]
        pltpu.make_async_copy(direct, direct, kv_recv.at[head]).wait()
        forward = remote(direct, passed, fwd_send.at[head], fwd_recv.at[head], partner)
        forward.start()
        pltpu.make_async_copy(qs.at[head], qs.at[head], q_recv.at[head]).wait()
        forward.wait()

        for kind, lag in enumerate(lags):

            @pl.when((lag > 0) & (head >= lag))
            def _():
                give_far(head - lag, kind)

        for at, group in ((outmost, (0, 1)), (facing, (2, 3, 4))):
            compute(head, at)
            for kind in group:

                @pl.when(lags[kind] == 0)
                def _():
                    give_far(head, kind)

        compute(head, near)
        give(head, near, 0)
        give(head, near, 1)
        compute(head, plane)
        give_plane(head)

    over_heads(attend)

    def give_rest(kind, begin, end):
        def body(head, carry):
            give_far(head, kind)
            return carry

        lax.fori_loop(begin, end, body, 0)

    for kind in range(3):
        give_rest(kind, heads - lags[kind], heads)
    give_rest(3, heads - lags[3], heads - LAST)
    give_rest(4, heads - lags[4], heads)
    give_rest(3, jnp.maximum(heads - lags[3], heads - LAST), heads)

    pltpu.make_async_copy(out_ref, out_ref, o_recv).wait()
    both = kv.at[:, :, pl.ds(0, (CHIPS - 1) * rows)]
    pltpu.make_async_copy(both, both, kv_send).wait()
    most = qs.at[:, pl.ds(0, (CORES * CHIPS - 1) * toks)]
    pltpu.make_async_copy(most, most, q_send).wait()
    pltpu.make_async_copy(most, most, o_send).wait()


def by_heads(keys, values, queries):
    nseq = lax.axis_size("seq")
    rows, width = keys.shape
    _, toks, _ = queries.shape
    heads = width // HEAD_DIM // CHIPS
    any_space = pl.BlockSpec(memory_space=pl.ANY)
    dma = pltpu.SemaphoreType.DMA
    return pl.pallas_call(
        functools.partial(attend_kernel, heads),
        out_shape=pltpu.VMEM(queries.shape, jnp.bfloat16),
        in_specs=[any_space] * 3,
        out_specs=pl.BlockSpec(memory_space=pltpu.VMEM),
        scratch_shapes=[
            pltpu.VMEM((heads, 2, nseq * rows, HEAD_DIM), jnp.bfloat16),
            pltpu.VMEM((heads, nseq * toks, HEAD_DIM), jnp.bfloat16),
            pltpu.VMEM((heads, nseq * toks, HEAD_DIM), jnp.bfloat16),
            dma, dma((heads,)), dma, dma((heads,)),
            dma((heads,)), dma((heads,)), dma, dma,
        ],
        compiler_params=pltpu.CompilerParams(collective_id=0, has_side_effects=True),
    )(keys, values, queries)


def by_groups(keys, values, queries):
    nseq = lax.axis_size("seq")
    blocks = nseq // GROUPS
    ctx_rows, width = keys.shape
    group_width = width // GROUPS
    heads_group = group_width // HEAD_DIM
    layers, tok_rows, _ = queries.shape
    query_total = tok_rows * nseq
    scale = 1.0 / math.sqrt(HEAD_DIM)

    def arrange(local_block):
        return local_block.reshape(ctx_rows // blocks, nseq, group_width)

    def by_source(array):
        return array.reshape((array.shape[0], blocks, GROUPS) + array.shape[2:])

    moved_keys, moved_values = (
        lax.all_to_all(arrange(keys), "seq", split_axis=1, concat_axis=1, tiled=True),
        lax.all_to_all(arrange(values), "seq", split_axis=1, concat_axis=1, tiled=True),
    )
    moved_keys = moved_keys.reshape(-1, group_width)
    moved_values = moved_values.reshape(-1, group_width)
    layer_outs = []
    for layer in range(layers):
        local_query = queries[layer]
        per_group = local_query.reshape(tok_rows, GROUPS, group_width)
        received = lax.all_to_all(
            jnp.broadcast_to(per_group[:, None], (tok_rows, blocks, GROUPS, group_width)).reshape(
                tok_rows, nseq, group_width
            ),
            "seq",
            split_axis=1,
            concat_axis=0,
            tiled=True,
        )
        own_block = received.reshape(query_total, group_width)

        def one_head(head):
            start = head * HEAD_DIM
            q_head = lax.dynamic_slice_in_dim(own_block, start, HEAD_DIM, 1)
            k_head = lax.dynamic_slice_in_dim(moved_keys, start, HEAD_DIM, 1)
            v_head = lax.dynamic_slice_in_dim(moved_values, start, HEAD_DIM, 1)
            scores = (
                lax.dot_general(
                    q_head, k_head, (((1,), (1,)), ((), ())), preferred_element_type=jnp.float32
                )
                * scale
            )
            peak = jnp.max(scores, axis=1)
            expo = jnp.exp(scores - peak[:, None])
            total = jnp.sum(expo, axis=1)
            summed = jnp.dot(expo.astype(jnp.bfloat16), v_head, preferred_element_type=jnp.float32)
            return (summed, peak, total)

        summed, peak, total = lax.map(one_head, jnp.arange(heads_group, dtype=jnp.int32))
        shaped = (
            summed.reshape(heads_group, nseq, tok_rows, HEAD_DIM),
            peak.reshape(heads_group, nseq, tok_rows),
            total.reshape(heads_group, nseq, tok_rows),
        )
        combine_summed = lax.all_to_all(shaped[0], "seq", split_axis=1, concat_axis=1, tiled=True)
        combine_peak = lax.all_to_all(shaped[1], "seq", split_axis=1, concat_axis=1, tiled=True)
        combine_total = lax.all_to_all(shaped[2], "seq", split_axis=1, concat_axis=1, tiled=True)
        rows = combine_peak.shape[2]
        summed_s = by_source(combine_summed)
        peak_s = by_source(combine_peak)
        total_s = by_source(combine_total)
        highest = jnp.max(peak_s, axis=1)
        factor = jnp.exp(peak_s - highest[:, None])
        denom = jnp.sum(factor * total_s, axis=1)
        numer = jnp.sum(factor[..., None] * summed_s, axis=1)
        result = numer / denom[..., None]
        result = jnp.transpose(result, (2, 1, 0, 3)).reshape(rows, GROUPS * heads_group * HEAD_DIM)
        mixed = result.astype(jnp.bfloat16)
        layer_outs.append(mixed)
    return jnp.stack(layer_outs)


def local(keys, values, queries):
    chips = lax.axis_size("seq") // CORES
    heads = keys.shape[1] // HEAD_DIM
    if chips == CHIPS and heads % chips == 0 and heads // chips > max(FIRST, LAST) and queries.shape[0] == CORES and queries.shape[1] % 16 == 0:
        return by_heads(keys, values, queries)
    return by_groups(keys, values, queries)


def solution(mesh):
    return jax.shard_map(
        local,
        mesh=mesh,
        in_specs=(P(("rep", "seq"), None), P(("rep", "seq"), None), P(None, ("rep", "seq"), None)),
        out_specs=P(None, ("rep", "seq"), None),
        check_vma=False,
    )
```

```python
import functools
import math

import jax
import jax.numpy as jnp
from jax import lax
from jax.experimental import pallas as pl
from jax.experimental.pallas import tpu as pltpu
from jax.sharding import PartitionSpec as P

HEAD_DIM = 128
GROUPS = 8
CORES = 2
SIDES = 2
PLANES = 4
CHIPS = PLANES * SIDES
LAGS = (
    ((3, 3, 3, 3), (0, 0, 0, 3), (0, 0, 3, 3), (0, 0, 4, 5)),
    ((3, 3, 3, 3), (0, 0, 0, 5), (0, 0, 3, 5), (0, 0, 4, 5)),
)
FIRST = 3
MESH = pl.DeviceIdType.MESH


def attend_kernel(heads, k_ref, v_ref, q_ref, out_ref, kv, qs, res, kv_send, kv_recv, q_send, q_recv,
                  fwd_send, fwd_recv, o_send, o_recv):
    rows = k_ref.shape[0]
    toks = q_ref.shape[1]
    group_width = heads * HEAD_DIM
    half = CHIPS * rows
    scale = 1.0 / math.sqrt(HEAD_DIM)
    rep = lax.axis_index("rep")
    me = lax.axis_index("seq")
    chip = lax.div(me, CORES)
    core = lax.rem(me, CORES)
    partner = me + 1 - 2 * core
    plane = lax.div(chip, SIDES)
    side = lax.rem(chip, SIDES)
    right = lax.div(plane, 2)
    inner = (plane == 1) | (plane == 2)
    outmost = 3 * (1 - right)
    facing = 2 - right
    near = 4 * right + 1 - plane

    def remote(src, dst, send, recv, target):
        return pltpu.make_async_remote_copy(
            src_ref=src, dst_ref=dst, send_sem=send, recv_sem=recv, device_id=(rep, target), device_id_type=MESH
        )

    def columns(owner, head):
        return pl.ds(pl.multiple_of(owner * group_width + head * HEAD_DIM, HEAD_DIM), HEAD_DIM)

    def chip_at(plane, side):
        return plane * SIDES + side

    my_rows = pl.ds(pl.multiple_of(chip * rows, rows), rows)
    my_toks = pl.ds(pl.multiple_of(me * toks, toks), toks)
    opposite = chip_at(facing, side)

    def send_rows(dest, head):
        cols = columns(dest, head)
        remote(k_ref.at[:, cols], kv.at[head, 0, my_rows], kv_send, kv_recv.at[head], CORES * dest + core).start()
        remote(v_ref.at[:, cols], kv.at[head, 1, my_rows], kv_send, kv_recv.at[head], CORES * dest + core).start()

    def send_queries(dest, head):
        cols = columns(dest, head)
        for layer in range(CORES):
            remote(q_ref.at[layer, :, cols], qs.at[head, my_toks], q_send, q_recv.at[head], CORES * dest + layer).start()

    def send_to(dest, head):
        send_rows(dest, head)
        send_queries(dest, head)

    def keep(head):
        cols = columns(chip, head)
        pltpu.make_async_copy(k_ref.at[:, cols], kv.at[head, 0, my_rows], kv_recv.at[head]).start()
        pltpu.make_async_copy(v_ref.at[:, cols], kv.at[head, 1, my_rows], kv_recv.at[head]).start()
        pltpu.make_async_copy(q_ref.at[core, :, cols], qs.at[head, my_toks], q_recv.at[head]).start()
        remote(q_ref.at[1 - core, :, cols], qs.at[head, my_toks], q_send, q_recv.at[head], partner).start()

    def over_heads(step, begin=0):
        def body(head, carry):
            step(head)
            return carry

        lax.fori_loop(begin, heads, body, 0)

    barrier = pltpu.get_barrier_semaphore()

    def greet(device):
        pl.semaphore_signal(barrier, inc=1, device_id=(rep, device), device_id_type=MESH)

    def greet_outer():
        for at in (0, PLANES - 1):
            for other in range(SIDES * CORES):
                greet(SIDES * CORES * at + other)

    @pl.when(inner)
    def _():
        greet(CORES * opposite + core)

        @pl.when(core == 1)
        def _():
            pl.semaphore_wait(barrier, 1)
            send_rows(opposite, 0)
            greet(partner)
            for head in range(1, FIRST):
                send_rows(opposite, head)
            pl.semaphore_wait(barrier, 1)

        @pl.when(core == 0)
        def _():
            pl.semaphore_wait(barrier, 2)
            greet(partner)
            for head in range(FIRST):
                send_rows(opposite, head)

        greet_outer()
        for head in range(FIRST):
            send_queries(opposite, head)
        over_heads(lambda head: send_to(opposite, head), FIRST)
        pl.semaphore_wait(barrier, 1)

    @pl.when(jnp.logical_not(inner))
    def _():
        for other in range(SIDES * CORES):
            greet(SIDES * CORES * outmost + other)
        for other in range(CORES):
            greet(CORES * chip_at(plane, 1 - side) + other)
        greet(partner)
        pl.semaphore_wait(barrier, CORES * CHIPS - 1)
        greet(CORES * chip_at(near, side) + core)

    def send_far(head):
        send_to(chip_at(outmost, 1 - side), head)
        send_to(chip_at(outmost, side), head)
        send_to(chip_at(facing, 1 - side), head)

        @pl.when(jnp.logical_not(inner))
        def _():
            send_to(opposite, head)

    def send_close(head):
        send_to(chip_at(near, 1 - side), head)
        send_to(chip_at(near, side), head)
        send_to(chip_at(plane, 1 - side), head)

    over_heads(send_far)
    over_heads(send_close)
    over_heads(keep)

    def block(head, device):
        return res.at[head, pl.ds(pl.multiple_of(device * toks, toks), toks)]

    def give(head, at, other, cores=(0, 1)):
        place = out_ref.at[core, :, columns(chip, head)]
        for where in cores:
            device = CORES * chip_at(at, other) + where
            remote(block(head, device), place, o_send, o_recv, device).start()

    kinds = (
        (outmost, 1 - side, (0, 1)),
        (outmost, side, (0, 1)),
        (facing, 1 - side, (1, 0)),
        (facing, side, (0,)),
        (facing, side, (1,)),
    )

    def give_far(head, kind):
        give(head, *kinds[kind])

    def give_plane(head):
        place = out_ref.at[core, :, columns(chip, head)]
        give(head, plane, 1 - side)
        remote(block(head, partner), place, o_send, o_recv, partner).start()
        pltpu.make_async_copy(block(head, me), place, o_recv).start()

    lags = [
        sum(
            min(LAGS[which][at][min(kind, 3)], heads) * jnp.where((plane == at) & (core == which), 1, 0)
            for which in range(CORES)
            for at in range(PLANES)
        )
        for kind in range(len(kinds))
    ]

    chunk = SIDES * CORES * toks

    def compute(head, at):
        part = pl.ds(pl.multiple_of(at * chunk, chunk), chunk)
        scores = lax.dot_general(
            qs[head, part], kv[head, 0], (((1,), (1,)), ((), ())), preferred_element_type=jnp.float32
        )
        peak = jnp.max(scores, axis=1, keepdims=True)
        expo = jnp.exp((scores - peak) * scale)
        total = jnp.sum(expo, axis=1, keepdims=True)
        summed = jnp.dot(expo.astype(jnp.bfloat16), kv[head, 1], preferred_element_type=jnp.float32)
        res[head, part] = (summed / total).astype(jnp.bfloat16)

    def attend(head):
        direct = kv.at[head, :, pl.ds(0, half)]
        passed = kv.at[head, :, pl.ds(half, half)]
        pltpu.make_async_copy(direct, direct, kv_recv.at[head]).wait()
        forward = remote(direct, passed, fwd_send.at[head], fwd_recv.at[head], partner)
        forward.start()
        pltpu.make_async_copy(qs.at[head], qs.at[head], q_recv.at[head]).wait()
        forward.wait()

        for kind, lag in enumerate(lags):

            @pl.when((lag > 0) & (head >= lag))
            def _():
                give_far(head - lag, kind)

        for at, group in ((outmost, (0, 1)), (facing, (2, 3, 4))):
            compute(head, at)
            for kind in group:

                @pl.when(lags[kind] == 0)
                def _():
                    give_far(head, kind)

        compute(head, near)
        give(head, near, 0)
        give(head, near, 1)
        compute(head, plane)
        give_plane(head)

    over_heads(attend)

    for kind, lag in enumerate(lags):
        over_heads(lambda head: give_far(head, kind), heads - lag)

    pltpu.make_async_copy(out_ref, out_ref, o_recv).wait()
    both = kv.at[:, :, pl.ds(0, (CHIPS - 1) * rows)]
    pltpu.make_async_copy(both, both, kv_send).wait()
    most = qs.at[:, pl.ds(0, (CORES * CHIPS - 1) * toks)]
    pltpu.make_async_copy(most, most, q_send).wait()
    pltpu.make_async_copy(most, most, o_send).wait()


def by_heads(keys, values, queries):
    nseq = lax.axis_size("seq")
    rows, width = keys.shape
    _, toks, _ = queries.shape
    heads = width // HEAD_DIM // CHIPS
    any_space = pl.BlockSpec(memory_space=pl.ANY)
    dma = pltpu.SemaphoreType.DMA
    return pl.pallas_call(
        functools.partial(attend_kernel, heads),
        out_shape=pltpu.VMEM(queries.shape, jnp.bfloat16),
        in_specs=[any_space] * 3,
        out_specs=pl.BlockSpec(memory_space=pltpu.VMEM),
        scratch_shapes=[
            pltpu.VMEM((heads, 2, nseq * rows, HEAD_DIM), jnp.bfloat16),
            pltpu.VMEM((heads, nseq * toks, HEAD_DIM), jnp.bfloat16),
            pltpu.VMEM((heads, nseq * toks, HEAD_DIM), jnp.bfloat16),
            dma, dma((heads,)), dma, dma((heads,)),
            dma((heads,)), dma((heads,)), dma, dma,
        ],
        compiler_params=pltpu.CompilerParams(collective_id=0, has_side_effects=True),
    )(keys, values, queries)


def by_groups(keys, values, queries):
    nseq = lax.axis_size("seq")
    blocks = nseq // GROUPS
    ctx_rows, width = keys.shape
    group_width = width // GROUPS
    heads_group = group_width // HEAD_DIM
    layers, tok_rows, _ = queries.shape
    query_total = tok_rows * nseq
    scale = 1.0 / math.sqrt(HEAD_DIM)

    def arrange(local_block):
        return local_block.reshape(ctx_rows // blocks, nseq, group_width)

    def by_source(array):
        return array.reshape((array.shape[0], blocks, GROUPS) + array.shape[2:])

    moved_keys, moved_values = (
        lax.all_to_all(arrange(keys), "seq", split_axis=1, concat_axis=1, tiled=True),
        lax.all_to_all(arrange(values), "seq", split_axis=1, concat_axis=1, tiled=True),
    )
    moved_keys = moved_keys.reshape(-1, group_width)
    moved_values = moved_values.reshape(-1, group_width)
    layer_outs = []
    for layer in range(layers):
        local_query = queries[layer]
        per_group = local_query.reshape(tok_rows, GROUPS, group_width)
        received = lax.all_to_all(
            jnp.broadcast_to(per_group[:, None], (tok_rows, blocks, GROUPS, group_width)).reshape(
                tok_rows, nseq, group_width
            ),
            "seq",
            split_axis=1,
            concat_axis=0,
            tiled=True,
        )
        own_block = received.reshape(query_total, group_width)

        def one_head(head):
            start = head * HEAD_DIM
            q_head = lax.dynamic_slice_in_dim(own_block, start, HEAD_DIM, 1)
            k_head = lax.dynamic_slice_in_dim(moved_keys, start, HEAD_DIM, 1)
            v_head = lax.dynamic_slice_in_dim(moved_values, start, HEAD_DIM, 1)
            scores = (
                lax.dot_general(
                    q_head, k_head, (((1,), (1,)), ((), ())), preferred_element_type=jnp.float32
                )
                * scale
            )
            peak = jnp.max(scores, axis=1)
            expo = jnp.exp(scores - peak[:, None])
            total = jnp.sum(expo, axis=1)
            summed = jnp.dot(expo.astype(jnp.bfloat16), v_head, preferred_element_type=jnp.float32)
            return (summed, peak, total)

        summed, peak, total = lax.map(one_head, jnp.arange(heads_group, dtype=jnp.int32))
        shaped = (
            summed.reshape(heads_group, nseq, tok_rows, HEAD_DIM),
            peak.reshape(heads_group, nseq, tok_rows),
            total.reshape(heads_group, nseq, tok_rows),
        )
        combine_summed = lax.all_to_all(shaped[0], "seq", split_axis=1, concat_axis=1, tiled=True)
        combine_peak = lax.all_to_all(shaped[1], "seq", split_axis=1, concat_axis=1, tiled=True)
        combine_total = lax.all_to_all(shaped[2], "seq", split_axis=1, concat_axis=1, tiled=True)
        rows = combine_peak.shape[2]
        summed_s = by_source(combine_summed)
        peak_s = by_source(combine_peak)
        total_s = by_source(combine_total)
        highest = jnp.max(peak_s, axis=1)
        factor = jnp.exp(peak_s - highest[:, None])
        denom = jnp.sum(factor * total_s, axis=1)
        numer = jnp.sum(factor[..., None] * summed_s, axis=1)
        result = numer / denom[..., None]
        result = jnp.transpose(result, (2, 1, 0, 3)).reshape(rows, GROUPS * heads_group * HEAD_DIM)
        mixed = result.astype(jnp.bfloat16)
        layer_outs.append(mixed)
    return jnp.stack(layer_outs)


def local(keys, values, queries):
    chips = lax.axis_size("seq") // CORES
    heads = keys.shape[1] // HEAD_DIM
    if chips == CHIPS and heads % chips == 0 and heads // chips > FIRST and queries.shape[0] == CORES and queries.shape[1] % 16 == 0:
        return by_heads(keys, values, queries)
    return by_groups(keys, values, queries)


def solution(mesh):
    return jax.shard_map(
        local,
        mesh=mesh,
        in_specs=(P(("rep", "seq"), None), P(("rep", "seq"), None), P(None, ("rep", "seq"), None)),
        out_specs=P(None, ("rep", "seq"), None),
        check_vma=False,
    )
```

```python
import functools
import math

import jax
import jax.numpy as jnp
from jax import lax
from jax.experimental import pallas as pl
from jax.experimental.pallas import tpu as pltpu
from jax.sharding import PartitionSpec as P

HEAD_DIM = 128
GROUPS = 8
CORES = 2
SIDES = 2
PLANES = 4
CHIPS = PLANES * SIDES
LAGS = (
    ((3, 3, 3, 3), (0, 0, 0, 3), (0, 0, 3, 3), (0, 0, 4, 5)),
    ((3, 3, 3, 3), (0, 0, 0, 5), (0, 0, 3, 5), (0, 0, 4, 5)),
)
LAST = 3
FIRST = 3
MESH = pl.DeviceIdType.MESH


def attend_kernel(heads, k_ref, v_ref, q_ref, out_ref, kv, qs, res, kv_send, kv_recv, q_send, q_recv,
                  fwd_send, fwd_recv, o_send, o_recv):
    rows = k_ref.shape[0]
    toks = q_ref.shape[1]
    group_width = heads * HEAD_DIM
    half = CHIPS * rows
    scale = 1.0 / math.sqrt(HEAD_DIM)
    rep = lax.axis_index("rep")
    me = lax.axis_index("seq")
    chip = lax.div(me, CORES)
    core = lax.rem(me, CORES)
    partner = me + 1 - 2 * core
    plane = lax.div(chip, SIDES)
    side = lax.rem(chip, SIDES)
    right = lax.div(plane, 2)
    inner = (plane == 1) | (plane == 2)
    outmost = 3 * (1 - right)
    facing = 2 - right
    near = 4 * right + 1 - plane

    def remote(src, dst, send, recv, target):
        return pltpu.make_async_remote_copy(
            src_ref=src, dst_ref=dst, send_sem=send, recv_sem=recv, device_id=(rep, target), device_id_type=MESH
        )

    def columns(owner, head):
        return pl.ds(pl.multiple_of(owner * group_width + head * HEAD_DIM, HEAD_DIM), HEAD_DIM)

    def chip_at(plane, side):
        return plane * SIDES + side

    my_rows = pl.ds(pl.multiple_of(chip * rows, rows), rows)
    my_toks = pl.ds(pl.multiple_of(me * toks, toks), toks)
    opposite = chip_at(facing, side)

    def send_rows(dest, head):
        cols = columns(dest, head)
        remote(k_ref.at[:, cols], kv.at[head, 0, my_rows], kv_send, kv_recv.at[head], CORES * dest + core).start()
        remote(v_ref.at[:, cols], kv.at[head, 1, my_rows], kv_send, kv_recv.at[head], CORES * dest + core).start()

    def send_queries(dest, head):
        cols = columns(dest, head)
        for layer in (1, 0):
            remote(q_ref.at[layer, :, cols], qs.at[head, my_toks], q_send, q_recv.at[head], CORES * dest + layer).start()

    def send_to(dest, head):
        send_rows(dest, head)
        send_queries(dest, head)

    def keep(head):
        cols = columns(chip, head)
        pltpu.make_async_copy(k_ref.at[:, cols], kv.at[head, 0, my_rows], kv_recv.at[head]).start()
        pltpu.make_async_copy(v_ref.at[:, cols], kv.at[head, 1, my_rows], kv_recv.at[head]).start()
        pltpu.make_async_copy(q_ref.at[core, :, cols], qs.at[head, my_toks], q_recv.at[head]).start()
        remote(q_ref.at[1 - core, :, cols], qs.at[head, my_toks], q_send, q_recv.at[head], partner).start()

    def over_heads(step, begin=0):
        def body(head, carry):
            step(head)
            return carry

        lax.fori_loop(begin, heads, body, 0)

    barrier = pltpu.get_barrier_semaphore()

    def greet(device):
        pl.semaphore_signal(barrier, inc=1, device_id=(rep, device), device_id_type=MESH)

    def greet_outer():
        for at in (0, PLANES - 1):
            for other in range(SIDES * CORES):
                greet(SIDES * CORES * at + other)

    @pl.when(inner)
    def _():
        greet(CORES * opposite + core)

        @pl.when(core == 1)
        def _():
            pl.semaphore_wait(barrier, 1)
            send_rows(opposite, 0)
            greet(partner)
            for head in range(1, FIRST):
                send_rows(opposite, head)
            pl.semaphore_wait(barrier, 1)

        @pl.when(core == 0)
        def _():
            pl.semaphore_wait(barrier, 2)
            greet(partner)
            for head in range(FIRST):
                send_rows(opposite, head)

        greet_outer()
        for head in range(FIRST):
            send_queries(opposite, head)
        over_heads(lambda head: send_to(opposite, head), FIRST)
        pl.semaphore_wait(barrier, 1)

    @pl.when(jnp.logical_not(inner))
    def _():
        for other in range(SIDES * CORES):
            greet(SIDES * CORES * outmost + other)
        for other in range(CORES):
            greet(CORES * chip_at(plane, 1 - side) + other)
        greet(partner)
        pl.semaphore_wait(barrier, CORES * CHIPS - 1)
        greet(CORES * chip_at(near, side) + core)

    def send_far(head):
        send_to(chip_at(outmost, 1 - side), head)
        send_to(chip_at(outmost, side), head)
        send_to(chip_at(facing, 1 - side), head)

        @pl.when(jnp.logical_not(inner))
        def _():
            send_to(opposite, head)

    def send_close(head):
        send_to(chip_at(near, 1 - side), head)
        send_to(chip_at(near, side), head)
        send_to(chip_at(plane, 1 - side), head)

    over_heads(send_far)
    over_heads(send_close)
    over_heads(keep)

    def block(head, device):
        return res.at[head, pl.ds(pl.multiple_of(device * toks, toks), toks)]

    def give(head, at, other, cores=(0, 1)):
        place = out_ref.at[core, :, columns(chip, head)]
        for where in cores:
            device = CORES * chip_at(at, other) + where
            remote(block(head, device), place, o_send, o_recv, device).start()

    kinds = (
        (outmost, 1 - side, (0, 1)),
        (outmost, side, (0, 1)),
        (facing, 1 - side, (1, 0)),
        (facing, side, (1,)),
        (facing, side, (0,)),
    )

    def give_far(head, kind):
        give(head, *kinds[kind])

    def give_plane(head):
        place = out_ref.at[core, :, columns(chip, head)]
        give(head, plane, 1 - side)
        remote(block(head, partner), place, o_send, o_recv, partner).start()
        pltpu.make_async_copy(block(head, me), place, o_recv).start()

    lags = [
        sum(
            min(LAGS[which][at][min(kind, 3)], heads) * jnp.where((plane == at) & (core == which), 1, 0)
            for which in range(CORES)
            for at in range(PLANES)
        )
        for kind in range(len(kinds))
    ]

    chunk = SIDES * CORES * toks

    def compute(head, at):
        part = pl.ds(pl.multiple_of(at * chunk, chunk), chunk)
        scores = lax.dot_general(
            qs[head, part], kv[head, 0], (((1,), (1,)), ((), ())), preferred_element_type=jnp.float32
        )
        peak = jnp.max(scores, axis=1, keepdims=True)
        expo = jnp.exp((scores - peak) * scale)
        total = jnp.sum(expo, axis=1, keepdims=True)
        summed = jnp.dot(expo.astype(jnp.bfloat16), kv[head, 1], preferred_element_type=jnp.float32)
        res[head, part] = (summed / total).astype(jnp.bfloat16)

    def attend(head):
        direct = kv.at[head, :, pl.ds(0, half)]
        passed = kv.at[head, :, pl.ds(half, half)]
        pltpu.make_async_copy(direct, direct, kv_recv.at[head]).wait()
        forward = remote(direct, passed, fwd_send.at[head], fwd_recv.at[head], partner)
        forward.start()
        pltpu.make_async_copy(qs.at[head], qs.at[head], q_recv.at[head]).wait()
        forward.wait()

        for kind, lag in enumerate(lags):

            @pl.when((lag > 0) & (head >= lag))
            def _():
                give_far(head - lag, kind)

        for at, group in ((outmost, (0, 1)), (facing, (2, 3, 4))):
            compute(head, at)
            for kind in group:

                @pl.when(lags[kind] == 0)
                def _():
                    give_far(head, kind)

        compute(head, near)
        give(head, near, 0)
        give(head, near, 1)
        compute(head, plane)
        give_plane(head)

    over_heads(attend)

    def give_rest(kind, begin, end):
        def body(head, carry):
            give_far(head, kind)
            return carry

        lax.fori_loop(begin, end, body, 0)

    for kind in range(3):
        give_rest(kind, heads - lags[kind], heads)
    give_rest(3, heads - lags[3], heads - LAST)
    give_rest(4, heads - lags[4], heads)
    give_rest(3, jnp.maximum(heads - lags[3], heads - LAST), heads)

    pltpu.make_async_copy(out_ref, out_ref, o_recv).wait()
    both = kv.at[:, :, pl.ds(0, (CHIPS - 1) * rows)]
    pltpu.make_async_copy(both, both, kv_send).wait()
    most = qs.at[:, pl.ds(0, (CORES * CHIPS - 1) * toks)]
    pltpu.make_async_copy(most, most, q_send).wait()
    pltpu.make_async_copy(most, most, o_send).wait()


def by_heads(keys, values, queries):
    nseq = lax.axis_size("seq")
    rows, width = keys.shape
    _, toks, _ = queries.shape
    heads = width // HEAD_DIM // CHIPS
    any_space = pl.BlockSpec(memory_space=pl.ANY)
    dma = pltpu.SemaphoreType.DMA
    return pl.pallas_call(
        functools.partial(attend_kernel, heads),
        out_shape=pltpu.VMEM(queries.shape, jnp.bfloat16),
        in_specs=[any_space] * 3,
        out_specs=pl.BlockSpec(memory_space=pltpu.VMEM),
        scratch_shapes=[
            pltpu.VMEM((heads, 2, nseq * rows, HEAD_DIM), jnp.bfloat16),
            pltpu.VMEM((heads, nseq * toks, HEAD_DIM), jnp.bfloat16),
            pltpu.VMEM((heads, nseq * toks, HEAD_DIM), jnp.bfloat16),
            dma, dma((heads,)), dma, dma((heads,)),
            dma((heads,)), dma((heads,)), dma, dma,
        ],
        compiler_params=pltpu.CompilerParams(collective_id=0, has_side_effects=True),
    )(keys, values, queries)


def by_groups(keys, values, queries):
    nseq = lax.axis_size("seq")
    blocks = nseq // GROUPS
    ctx_rows, width = keys.shape
    group_width = width // GROUPS
    heads_group = group_width // HEAD_DIM
    layers, tok_rows, _ = queries.shape
    query_total = tok_rows * nseq
    scale = 1.0 / math.sqrt(HEAD_DIM)

    def arrange(local_block):
        return local_block.reshape(ctx_rows // blocks, nseq, group_width)

    def by_source(array):
        return array.reshape((array.shape[0], blocks, GROUPS) + array.shape[2:])

    moved_keys, moved_values = (
        lax.all_to_all(arrange(keys), "seq", split_axis=1, concat_axis=1, tiled=True),
        lax.all_to_all(arrange(values), "seq", split_axis=1, concat_axis=1, tiled=True),
    )
    moved_keys = moved_keys.reshape(-1, group_width)
    moved_values = moved_values.reshape(-1, group_width)
    layer_outs = []
    for layer in range(layers):
        local_query = queries[layer]
        per_group = local_query.reshape(tok_rows, GROUPS, group_width)
        received = lax.all_to_all(
            jnp.broadcast_to(per_group[:, None], (tok_rows, blocks, GROUPS, group_width)).reshape(
                tok_rows, nseq, group_width
            ),
            "seq",
            split_axis=1,
            concat_axis=0,
            tiled=True,
        )
        own_block = received.reshape(query_total, group_width)

        def one_head(head):
            start = head * HEAD_DIM
            q_head = lax.dynamic_slice_in_dim(own_block, start, HEAD_DIM, 1)
            k_head = lax.dynamic_slice_in_dim(moved_keys, start, HEAD_DIM, 1)
            v_head = lax.dynamic_slice_in_dim(moved_values, start, HEAD_DIM, 1)
            scores = (
                lax.dot_general(
                    q_head, k_head, (((1,), (1,)), ((), ())), preferred_element_type=jnp.float32
                )
                * scale
            )
            peak = jnp.max(scores, axis=1)
            expo = jnp.exp(scores - peak[:, None])
            total = jnp.sum(expo, axis=1)
            summed = jnp.dot(expo.astype(jnp.bfloat16), v_head, preferred_element_type=jnp.float32)
            return (summed, peak, total)

        summed, peak, total = lax.map(one_head, jnp.arange(heads_group, dtype=jnp.int32))
        shaped = (
            summed.reshape(heads_group, nseq, tok_rows, HEAD_DIM),
            peak.reshape(heads_group, nseq, tok_rows),
            total.reshape(heads_group, nseq, tok_rows),
        )
        combine_summed = lax.all_to_all(shaped[0], "seq", split_axis=1, concat_axis=1, tiled=True)
        combine_peak = lax.all_to_all(shaped[1], "seq", split_axis=1, concat_axis=1, tiled=True)
        combine_total = lax.all_to_all(shaped[2], "seq", split_axis=1, concat_axis=1, tiled=True)
        rows = combine_peak.shape[2]
        summed_s = by_source(combine_summed)
        peak_s = by_source(combine_peak)
        total_s = by_source(combine_total)
        highest = jnp.max(peak_s, axis=1)
        factor = jnp.exp(peak_s - highest[:, None])
        denom = jnp.sum(factor * total_s, axis=1)
        numer = jnp.sum(factor[..., None] * summed_s, axis=1)
        result = numer / denom[..., None]
        result = jnp.transpose(result, (2, 1, 0, 3)).reshape(rows, GROUPS * heads_group * HEAD_DIM)
        mixed = result.astype(jnp.bfloat16)
        layer_outs.append(mixed)
    return jnp.stack(layer_outs)


def local(keys, values, queries):
    chips = lax.axis_size("seq") // CORES
    heads = keys.shape[1] // HEAD_DIM
    if chips == CHIPS and heads % chips == 0 and heads // chips > max(FIRST, LAST) and queries.shape[0] == CORES and queries.shape[1] % 16 == 0:
        return by_heads(keys, values, queries)
    return by_groups(keys, values, queries)


def solution(mesh):
    return jax.shard_map(
        local,
        mesh=mesh,
        in_specs=(P(("rep", "seq"), None), P(("rep", "seq"), None), P(None, ("rep", "seq"), None)),
        out_specs=P(None, ("rep", "seq"), None),
        check_vma=False,
    )
```

```python
import functools
import math

import jax
import jax.numpy as jnp
from jax import lax
from jax.experimental import pallas as pl
from jax.experimental.pallas import tpu as pltpu
from jax.sharding import PartitionSpec as P

HEAD_DIM = 128
GROUPS = 8
CORES = 2
SIDES = 2
PLANES = 4
CHIPS = PLANES * SIDES
LAGS = (
    ((3, 3, 3, 3), (0, 0, 0, 3), (0, 0, 3, 3), (0, 0, 4, 5)),
    ((3, 3, 3, 3), (0, 0, 0, 5), (0, 0, 3, 5), (0, 0, 4, 5)),
)
LAST = 4
FIRST = 3
MESH = pl.DeviceIdType.MESH


def attend_kernel(heads, k_ref, v_ref, q_ref, out_ref, kv, qs, res, kv_send, kv_recv, q_send, q_recv,
                  fwd_send, fwd_recv, o_send, o_recv):
    rows = k_ref.shape[0]
    toks = q_ref.shape[1]
    group_width = heads * HEAD_DIM
    half = CHIPS * rows
    scale = 1.0 / math.sqrt(HEAD_DIM)
    rep = lax.axis_index("rep")
    me = lax.axis_index("seq")
    chip = lax.div(me, CORES)
    core = lax.rem(me, CORES)
    partner = me + 1 - 2 * core
    plane = lax.div(chip, SIDES)
    side = lax.rem(chip, SIDES)
    right = lax.div(plane, 2)
    inner = (plane == 1) | (plane == 2)
    outmost = 3 * (1 - right)
    facing = 2 - right
    near = 4 * right + 1 - plane

    def remote(src, dst, send, recv, target):
        return pltpu.make_async_remote_copy(
            src_ref=src, dst_ref=dst, send_sem=send, recv_sem=recv, device_id=(rep, target), device_id_type=MESH
        )

    def columns(owner, head):
        return pl.ds(pl.multiple_of(owner * group_width + head * HEAD_DIM, HEAD_DIM), HEAD_DIM)

    def chip_at(plane, side):
        return plane * SIDES + side

    my_rows = pl.ds(pl.multiple_of(chip * rows, rows), rows)
    my_toks = pl.ds(pl.multiple_of(me * toks, toks), toks)
    opposite = chip_at(facing, side)

    def send_rows(dest, head):
        cols = columns(dest, head)
        remote(k_ref.at[:, cols], kv.at[head, 0, my_rows], kv_send, kv_recv.at[head], CORES * dest + core).start()
        remote(v_ref.at[:, cols], kv.at[head, 1, my_rows], kv_send, kv_recv.at[head], CORES * dest + core).start()

    def send_queries(dest, head):
        cols = columns(dest, head)
        for layer in range(CORES):
            remote(q_ref.at[layer, :, cols], qs.at[head, my_toks], q_send, q_recv.at[head], CORES * dest + layer).start()

    def send_to(dest, head):
        send_rows(dest, head)
        send_queries(dest, head)

    def keep(head):
        cols = columns(chip, head)
        pltpu.make_async_copy(k_ref.at[:, cols], kv.at[head, 0, my_rows], kv_recv.at[head]).start()
        pltpu.make_async_copy(v_ref.at[:, cols], kv.at[head, 1, my_rows], kv_recv.at[head]).start()
        pltpu.make_async_copy(q_ref.at[core, :, cols], qs.at[head, my_toks], q_recv.at[head]).start()
        remote(q_ref.at[1 - core, :, cols], qs.at[head, my_toks], q_send, q_recv.at[head], partner).start()

    def over_heads(step, begin=0):
        def body(head, carry):
            step(head)
            return carry

        lax.fori_loop(begin, heads, body, 0)

    barrier = pltpu.get_barrier_semaphore()

    def greet(device):
        pl.semaphore_signal(barrier, inc=1, device_id=(rep, device), device_id_type=MESH)

    def greet_outer():
        for at in (0, PLANES - 1):
            for other in range(SIDES * CORES):
                greet(SIDES * CORES * at + other)

    @pl.when(inner)
    def _():
        greet(CORES * opposite + core)

        @pl.when(core == 1)
        def _():
            pl.semaphore_wait(barrier, 1)
            greet(partner)
            for head in range(FIRST):
                send_rows(opposite, head)
            pl.semaphore_wait(barrier, 1)

        @pl.when(core == 0)
        def _():
            pl.semaphore_wait(barrier, 2)
            greet(partner)
            for head in range(FIRST):
                send_rows(opposite, head)

        greet_outer()
        for head in range(FIRST):
            send_queries(opposite, head)
        over_heads(lambda head: send_to(opposite, head), FIRST)
        pl.semaphore_wait(barrier, 1)

    @pl.when(jnp.logical_not(inner))
    def _():
        for other in range(SIDES * CORES):
            greet(SIDES * CORES * outmost + other)
        for other in range(CORES):
            greet(CORES * chip_at(plane, 1 - side) + other)
        greet(partner)
        pl.semaphore_wait(barrier, CORES * CHIPS - 1)
        greet(CORES * chip_at(near, side) + core)

    def send_far(head):
        send_to(chip_at(outmost, 1 - side), head)
        send_to(chip_at(outmost, side), head)
        send_to(chip_at(facing, 1 - side), head)

        @pl.when(jnp.logical_not(inner))
        def _():
            send_to(opposite, head)

    def send_close(head):
        send_to(chip_at(near, 1 - side), head)
        send_to(chip_at(near, side), head)
        send_to(chip_at(plane, 1 - side), head)

    over_heads(send_far)
    over_heads(send_close)
    over_heads(keep)

    def block(head, device):
        return res.at[head, pl.ds(pl.multiple_of(device * toks, toks), toks)]

    def give(head, at, other, cores=(0, 1)):
        place = out_ref.at[core, :, columns(chip, head)]
        for where in cores:
            device = CORES * chip_at(at, other) + where
            remote(block(head, device), place, o_send, o_recv, device).start()

    kinds = (
        (outmost, 1 - side, (0, 1)),
        (outmost, side, (0, 1)),
        (facing, 1 - side, (1, 0)),
        (facing, side, (1,)),
        (facing, side, (0,)),
    )

    def give_far(head, kind):
        give(head, *kinds[kind])

    def give_plane(head):
        place = out_ref.at[core, :, columns(chip, head)]
        give(head, plane, 1 - side)
        remote(block(head, partner), place, o_send, o_recv, partner).start()
        pltpu.make_async_copy(block(head, me), place, o_recv).start()

    lags = [
        sum(
            min(LAGS[which][at][min(kind, 3)], heads) * jnp.where((plane == at) & (core == which), 1, 0)
            for which in range(CORES)
            for at in range(PLANES)
        )
        for kind in range(len(kinds))
    ]

    chunk = SIDES * CORES * toks

    def compute(head, at):
        part = pl.ds(pl.multiple_of(at * chunk, chunk), chunk)
        scores = lax.dot_general(
            qs[head, part], kv[head, 0], (((1,), (1,)), ((), ())), preferred_element_type=jnp.float32
        )
        peak = jnp.max(scores, axis=1, keepdims=True)
        expo = jnp.exp((scores - peak) * scale)
        total = jnp.sum(expo, axis=1, keepdims=True)
        summed = jnp.dot(expo.astype(jnp.bfloat16), kv[head, 1], preferred_element_type=jnp.float32)
        res[head, part] = (summed / total).astype(jnp.bfloat16)

    def attend(head):
        direct = kv.at[head, :, pl.ds(0, half)]
        passed = kv.at[head, :, pl.ds(half, half)]
        pltpu.make_async_copy(direct, direct, kv_recv.at[head]).wait()
        forward = remote(direct, passed, fwd_send.at[head], fwd_recv.at[head], partner)
        forward.start()
        pltpu.make_async_copy(qs.at[head], qs.at[head], q_recv.at[head]).wait()
        forward.wait()

        for kind, lag in enumerate(lags):

            @pl.when((lag > 0) & (head >= lag))
            def _():
                give_far(head - lag, kind)

        for at, group in ((outmost, (0, 1)), (facing, (2, 3, 4))):
            compute(head, at)
            for kind in group:

                @pl.when(lags[kind] == 0)
                def _():
                    give_far(head, kind)

        compute(head, near)
        give(head, near, 0)
        give(head, near, 1)
        compute(head, plane)
        give_plane(head)

    over_heads(attend)

    def give_rest(kind, begin, end):
        def body(head, carry):
            give_far(head, kind)
            return carry

        lax.fori_loop(begin, end, body, 0)

    for kind in range(3):
        give_rest(kind, heads - lags[kind], heads)
    give_rest(3, heads - lags[3], heads - LAST)
    give_rest(4, heads - lags[4], heads)
    give_rest(3, jnp.maximum(heads - lags[3], heads - LAST), heads)

    pltpu.make_async_copy(out_ref, out_ref, o_recv).wait()
    both = kv.at[:, :, pl.ds(0, (CHIPS - 1) * rows)]
    pltpu.make_async_copy(both, both, kv_send).wait()
    most = qs.at[:, pl.ds(0, (CORES * CHIPS - 1) * toks)]
    pltpu.make_async_copy(most, most, q_send).wait()
    pltpu.make_async_copy(most, most, o_send).wait()


def by_heads(keys, values, queries):
    nseq = lax.axis_size("seq")
    rows, width = keys.shape
    _, toks, _ = queries.shape
    heads = width // HEAD_DIM // CHIPS
    any_space = pl.BlockSpec(memory_space=pl.ANY)
    dma = pltpu.SemaphoreType.DMA
    return pl.pallas_call(
        functools.partial(attend_kernel, heads),
        out_shape=pltpu.VMEM(queries.shape, jnp.bfloat16),
        in_specs=[any_space] * 3,
        out_specs=pl.BlockSpec(memory_space=pltpu.VMEM),
        scratch_shapes=[
            pltpu.VMEM((heads, 2, nseq * rows, HEAD_DIM), jnp.bfloat16),
            pltpu.VMEM((heads, nseq * toks, HEAD_DIM), jnp.bfloat16),
            pltpu.VMEM((heads, nseq * toks, HEAD_DIM), jnp.bfloat16),
            dma, dma((heads,)), dma, dma((heads,)),
            dma((heads,)), dma((heads,)), dma, dma,
        ],
        compiler_params=pltpu.CompilerParams(collective_id=0, has_side_effects=True),
    )(keys, values, queries)


def by_groups(keys, values, queries):
    nseq = lax.axis_size("seq")
    blocks = nseq // GROUPS
    ctx_rows, width = keys.shape
    group_width = width // GROUPS
    heads_group = group_width // HEAD_DIM
    layers, tok_rows, _ = queries.shape
    query_total = tok_rows * nseq
    scale = 1.0 / math.sqrt(HEAD_DIM)

    def arrange(local_block):
        return local_block.reshape(ctx_rows // blocks, nseq, group_width)

    def by_source(array):
        return array.reshape((array.shape[0], blocks, GROUPS) + array.shape[2:])

    moved_keys, moved_values = (
        lax.all_to_all(arrange(keys), "seq", split_axis=1, concat_axis=1, tiled=True),
        lax.all_to_all(arrange(values), "seq", split_axis=1, concat_axis=1, tiled=True),
    )
    moved_keys = moved_keys.reshape(-1, group_width)
    moved_values = moved_values.reshape(-1, group_width)
    layer_outs = []
    for layer in range(layers):
        local_query = queries[layer]
        per_group = local_query.reshape(tok_rows, GROUPS, group_width)
        received = lax.all_to_all(
            jnp.broadcast_to(per_group[:, None], (tok_rows, blocks, GROUPS, group_width)).reshape(
                tok_rows, nseq, group_width
            ),
            "seq",
            split_axis=1,
            concat_axis=0,
            tiled=True,
        )
        own_block = received.reshape(query_total, group_width)

        def one_head(head):
            start = head * HEAD_DIM
            q_head = lax.dynamic_slice_in_dim(own_block, start, HEAD_DIM, 1)
            k_head = lax.dynamic_slice_in_dim(moved_keys, start, HEAD_DIM, 1)
            v_head = lax.dynamic_slice_in_dim(moved_values, start, HEAD_DIM, 1)
            scores = (
                lax.dot_general(
                    q_head, k_head, (((1,), (1,)), ((), ())), preferred_element_type=jnp.float32
                )
                * scale
            )
            peak = jnp.max(scores, axis=1)
            expo = jnp.exp(scores - peak[:, None])
            total = jnp.sum(expo, axis=1)
            summed = jnp.dot(expo.astype(jnp.bfloat16), v_head, preferred_element_type=jnp.float32)
            return (summed, peak, total)

        summed, peak, total = lax.map(one_head, jnp.arange(heads_group, dtype=jnp.int32))
        shaped = (
            summed.reshape(heads_group, nseq, tok_rows, HEAD_DIM),
            peak.reshape(heads_group, nseq, tok_rows),
            total.reshape(heads_group, nseq, tok_rows),
        )
        combine_summed = lax.all_to_all(shaped[0], "seq", split_axis=1, concat_axis=1, tiled=True)
        combine_peak = lax.all_to_all(shaped[1], "seq", split_axis=1, concat_axis=1, tiled=True)
        combine_total = lax.all_to_all(shaped[2], "seq", split_axis=1, concat_axis=1, tiled=True)
        rows = combine_peak.shape[2]
        summed_s = by_source(combine_summed)
        peak_s = by_source(combine_peak)
        total_s = by_source(combine_total)
        highest = jnp.max(peak_s, axis=1)
        factor = jnp.exp(peak_s - highest[:, None])
        denom = jnp.sum(factor * total_s, axis=1)
        numer = jnp.sum(factor[..., None] * summed_s, axis=1)
        result = numer / denom[..., None]
        result = jnp.transpose(result, (2, 1, 0, 3)).reshape(rows, GROUPS * heads_group * HEAD_DIM)
        mixed = result.astype(jnp.bfloat16)
        layer_outs.append(mixed)
    return jnp.stack(layer_outs)


def local(keys, values, queries):
    chips = lax.axis_size("seq") // CORES
    heads = keys.shape[1] // HEAD_DIM
    if chips == CHIPS and heads % chips == 0 and heads // chips > max(FIRST, LAST) and queries.shape[0] == CORES and queries.shape[1] % 16 == 0:
        return by_heads(keys, values, queries)
    return by_groups(keys, values, queries)


def solution(mesh):
    return jax.shard_map(
        local,
        mesh=mesh,
        in_specs=(P(("rep", "seq"), None), P(("rep", "seq"), None), P(None, ("rep", "seq"), None)),
        out_specs=P(None, ("rep", "seq"), None),
        check_vma=False,
    )
```
